512 devices in a mesh: grid: 4 (over z_lo), gx: 16 (over x, y), gy: 8 (over z_hi, core).
Axes of the slice: x: 4, y: 4, z: 16 (z_hi: 4, z_lo: 4; z = z_hi * 4 + z_lo), core: 2. Of those that a mesh axis runs over, the one named last changes fastest.
Arguments:
- adjoint: float32 [4, 24, 512, 2048], P('grid', None, 'gx', 'gy'), may hold values from -6 to 6
- sea_mask: int32 [4, 512, 2048], P('grid', 'gx', 'gy'), may hold values 0 or 1
- diffusivity: float32 [4, 512, 2048], P('grid', 'gx', 'gy'), may hold values from 0.03 to 0.24
- aggregation: float32 [4, 512, 2048], P('grid', 'gx', 'gy'), may hold values from 0.02 to 0.3
- breakup: float32 [4, 512, 2048], P('grid', 'gx', 'gy'), may hold values from 0.02 to 0.3
- sponge: float32 [4, 512, 2048], P('grid', 'gx', 'gy'), may hold values from 0.05 to 0.6
- settling: float32 [4, 3], replicated, may hold values from 0.05 to 0.5
- partner_flip: int32 [3, 16, 8], replicated, may hold values from 0 to 1
- row_offset: int32 [3, 16, 8], replicated, may hold values from 0 to 16
- col_offset: int32 [3, 16, 8], replicated, may hold values from 0 to 128
Outputs:
- adjoint_out: float32 [4, 24, 512, 2048], P('grid', None, 'gx', 'gy')
The draws below stay inside these ranges and needn't reach their ends.
Inputs may be any that keep to these rules, and one draw needn't show every extreme that they name: `partner_flip`: every child tile is paired with exactly one parent tile in its own tile column, in its own tile row or the row whose index differs in the lowest bit; a parent tile serves 0 to 6 child tiles. `row_offset`: the footprint lies inside the paired parent tile. `col_offset`: the footprint lies inside the paired parent tile.
All inputs are finite; a program needn't handle non-finite values. No bound on the sum of `sea_mask` on one device may be relied on, other than what follows from the above.
Results may differ from the reference program's by a relative error of at most 0.0001.
Values sent between devices are 32-bit elements; how exact they have to be, the bound alone decides.
A program may use at most 64 MiB of HBM per device.

```python
import math
import jax
import jax.numpy as jnp
from jax import lax

NCLS = 3
LEV = 8
STEPS = 2
CR = 32
CC = 256
K = 24
NR = 512
NC = 2048
N_GRID = 4
N_GX = 16
N_GY = 8


def place_ends(drawn, rng, least, largest):
    shape = drawn.shape
    index_at = [jax.random.randint(jax.random.fold_in(rng, axis), (), 0, shape[axis]) for axis in range(len(shape))]
    drawn = drawn.at[tuple(index_at)].set(least)
    longest = shape.index(max(shape))
    index_at[longest] = (index_at[longest] + 1) % shape[longest]
    return drawn.at[tuple(index_at)].set(largest)


def shard_levels(rng, shape, cuts, least, largest):
    def one(dim, blocks):
        heights = jax.random.uniform(jax.random.fold_in(jax.random.fold_in(rng, 6), dim), (blocks,), jnp.float32, least / len(cuts), largest / len(cuts))
        return jnp.repeat(jnp.exp(heights), shape[dim] // blocks).reshape((-1,) + (1,) * (len(shape) - dim - 1))

    loudness = one(*cuts[0])
    for cut in cuts[1:]:
        loudness = loudness * one(*cut)
    return loudness


def centred(own_key, shape, deviation, bound, shards=(), kind=jnp.bfloat16):
    entries = deviation * jax.random.normal(own_key, shape, jnp.float32)
    if shards:
        entries = entries * shard_levels(own_key, shape, shards, -0.22, 0.18)
    return jnp.clip(entries, -bound, bound).astype(kind)


def setup_inputs(seed: int = 0) -> dict:
    key_list = jax.random.split(jax.random.key(seed), 11)
    return {
        "adjoint": centred(key_list[0], (N_GRID, K, NR, NC), 1.0, 6.0, ((0, 4), (2, 16), (3, 8)), jnp.float32),
        "sea_mask": place_ends((jax.random.randint(key_list[1], (N_GRID, NR, NC), 0, 5) < 4).astype(jnp.int32), jax.random.fold_in(key_list[1], 1), 0, 1),
        "diffusivity": jnp.clip(0.03 + 0.21 * jax.random.uniform(key_list[2], (N_GRID, NR, NC), jnp.float32) ** shard_levels(key_list[2], (N_GRID, NR, NC), ((0, 4), (1, 16), (2, 8)), -0.2, 0.2), 0.03, 0.24),
        "aggregation": jnp.clip(jnp.exp(math.log(0.3) - 2.7080503 * jax.random.uniform(key_list[3], (N_GRID, NR, NC), jnp.float32) ** shard_levels(key_list[3], (N_GRID, NR, NC), ((0, 4), (1, 16), (2, 8)), -0.2, 0.2)), 0.02, 0.3),
        "breakup": jnp.clip(jnp.exp(math.log(0.3) - 2.7080503 * jax.random.uniform(key_list[4], (N_GRID, NR, NC), jnp.float32) ** shard_levels(key_list[4], (N_GRID, NR, NC), ((0, 4), (1, 16), (2, 8)), -0.2, 0.2)), 0.02, 0.3),
        "sponge": jnp.clip(0.05 + 0.55 * jax.random.uniform(key_list[5], (N_GRID, NR, NC), jnp.float32) ** shard_levels(key_list[5], (N_GRID, NR, NC), ((0, 4), (1, 16), (2, 8)), -0.2, 0.2), 0.05, 0.6),
        "settling": jnp.clip(jnp.exp(jax.random.uniform(key_list[6], (N_GRID, NCLS), jnp.float32, math.log(0.05), math.log(0.5))), 0.05, 0.5),
        "partner_flip": place_ends(jax.random.randint(key_list[7], (N_GRID - 1, N_GX, N_GY), 0, 2), jax.random.fold_in(key_list[7], 1), 0, 1).astype(jnp.int32),
        "row_offset": place_ends(jax.random.randint(key_list[8], (N_GRID - 1, N_GX, N_GY), 0, CR // 2 + 1), jax.random.fold_in(key_list[8], 1), 0, (CR // 2 + 1) - 1).astype(jnp.int32),
        "col_offset": place_ends(jax.random.randint(key_list[9], (N_GRID - 1, N_GX, N_GY), 0, CC // 2 + 1), jax.random.fold_in(key_list[9], 1), 0, (CC // 2 + 1) - 1).astype(jnp.int32),
    }


relaxation = 0.125


def block_sums(values):
    shape = values.shape
    return values.reshape(shape[:-2] + (shape[-2] // 2, 2, shape[-1] // 2, 2)).sum(axis=(-3, -1))


def expand_cells(values):
    return jnp.repeat(jnp.repeat(values, 2, axis=-2), 2, axis=-1)


def swap_pairs(values, axis):
    shape = values.shape
    split = values.reshape(shape[:axis] + (shape[axis] // 2, 2) + shape[axis + 1:])
    return jnp.flip(split, axis + 1).reshape(shape)


def nest_adjoint(state, sponge, partner_flip, row_offset, col_offset):
    half_r = CR // 2
    half_c = CC // 2
    parent = state[0].reshape(K, N_GX, CR, N_GY, CC).transpose(1, 3, 0, 2, 4)
    children = state[1:].reshape(N_GRID - 1, K, N_GX, CR, N_GY, CC).transpose(0, 2, 4, 1, 3, 5)
    weights = sponge[1:].reshape(N_GRID - 1, N_GX, CR, N_GY, CC).transpose(0, 1, 3, 2, 4)
    flips = partner_flip[..., None, None, None]
    source = jnp.where(flips == 0, parent[None], swap_pairs(parent, 0)[None])
    number = (N_GRID - 1) * N_GX * N_GY
    tops = row_offset.reshape(number).astype(jnp.int32)
    lefts = col_offset.reshape(number).astype(jnp.int32)
    anchor = jnp.zeros((), jnp.int32)

    def cut_block(block, top_row, left_col):
        return lax.dynamic_slice(block, (anchor, top_row, left_col), (K, half_r, half_c))

    prints = jax.vmap(cut_block)(source.reshape(number, K, CR, CC), tops, lefts)
    prints = prints.reshape(N_GRID - 1, N_GX, N_GY, K, half_r, half_c)
    new_children = (1.0 - weights[:, :, :, None]) * children + (relaxation / 4.0) * expand_cells(prints)
    sent = block_sums(weights[:, :, :, None] * children).reshape(number, K, half_r, half_c)

    def place_block(piece, top_row, left_col):
        return lax.dynamic_update_slice(jnp.zeros((K, CR, CC), jnp.float32), piece, (anchor, top_row, left_col))

    def cover_block(top_row, left_col):
        return lax.dynamic_update_slice(jnp.zeros((CR, CC), jnp.float32), jnp.ones((half_r, half_c), jnp.float32), (top_row, left_col))

    placed = jax.vmap(place_block)(sent, tops, lefts).reshape(N_GRID - 1, N_GX, N_GY, K, CR, CC)
    boxes = jax.vmap(cover_block)(tops, lefts).reshape(N_GRID - 1, N_GX, N_GY, CR, CC)
    same = (partner_flip == 0).astype(jnp.float32)
    cross = (partner_flip == 1).astype(jnp.float32)
    gathered = jnp.sum(placed * same[..., None, None, None] + swap_pairs(placed * cross[..., None, None, None], 1), axis=0)
    covered = jnp.sum(boxes * same[..., None, None] + swap_pairs(boxes * cross[..., None, None], 1), axis=0)
    new_parent = (1.0 - relaxation * covered[:, :, None]) * parent + gathered
    parent_back = new_parent.transpose(2, 0, 3, 1, 4).reshape(K, N_GX * CR, N_GY * CC)
    children_back = new_children.transpose(0, 3, 1, 4, 2, 5).reshape(N_GRID - 1, K, N_GX * CR, N_GY * CC)
    return jnp.concatenate([parent_back[None], children_back], axis=0)


def floc_adjoint(values, aggregation, breakup):
    shape = values.shape
    split = values.reshape((shape[0], NCLS, LEV) + shape[2:])
    agg = aggregation[:, None]
    brk = breakup[:, None]
    first = split[:, 0]
    second = split[:, 1]
    third = split[:, 2]
    new_first = (1.0 - agg) * first + agg * second
    new_second = brk * first + (1.0 - agg - brk) * second + agg * third
    new_third = brk * second + (1.0 - brk) * third
    return jnp.stack([new_first, new_second, new_third], axis=1).reshape(shape)


def settle_adjoint(values, rates):
    shape = values.shape
    split = values.reshape((shape[0], NCLS, LEV) + shape[2:])
    below = jnp.concatenate([split[:, :, 1:], jnp.zeros_like(split[:, :, :1])], axis=2)
    speed = rates[:, :, None, None, None]
    return ((1.0 - speed) * split + speed * below).reshape(shape)


def reference(adjoint, sea_mask, diffusivity, aggregation, breakup, sponge, settling, partner_flip, row_offset, col_offset):
    state = adjoint
    for step_number in range(STEPS):
        state = nest_adjoint(state, sponge, partner_flip, row_offset, col_offset)
        state = floc_adjoint(state, aggregation, breakup)
        state = settle_adjoint(state, settling)
        wet = sea_mask.astype(jnp.float32)[:, None] * state
        flux = diffusivity[:, None] * wet
        padded = jnp.pad(flux, ((0, 0), (0, 0), (1, 1), (1, 1)))
        state = wet + padded[:, :, :-2, 1:-1] + padded[:, :, 2:, 1:-1] + padded[:, :, 1:-1, :-2] + padded[:, :, 1:-1, 2:] - 4.0 * flux
    return state
```

```python
import functools

import jax
import jax.numpy as jnp
from jax import lax
from jax.experimental import pallas as pl
from jax.experimental.pallas import tpu as pltpu
from jax.sharding import PartitionSpec as P

NCLS = 3
LEV = 8
STEPS = 2
CR = 32
CC = 256
HR = 16
HC = 128
SLOTS = 3
relaxation = 0.125

CHUNKS = 4
NL = LEV // CHUNKS
NK = NL * NCLS
NKP = -(-NK // 8) * 8
ROWS = NK * CR
WIDE = -(-ROWS // 128) * 128
TRIPS = STEPS * CHUNKS
MESH = pl.DeviceIdType.MESH
F32 = jnp.float32
BF16 = jnp.bfloat16

NORTH, SOUTH, WEST, EAST, UP, DOWN_X, UP_X, DOWN = 0, 1, 2, 3, 4, 7, 8, 9
KINDS = 12


def iota(shape, dim):
    return lax.broadcasted_iota(jnp.int32, shape, dim)


def halves(x):
    high = x.astype(BF16)
    return high, (x - high.astype(F32)).astype(BF16)


def exact_dot(x, selector):
    high, low = halves(x)
    return jnp.dot(high, selector, preferred_element_type=F32) + jnp.dot(low, selector, preferred_element_type=F32)


def kernel(
    adjoint,
    sea_mask,
    diffusivity,
    aggregation,
    breakup,
    sponge,
    settling,
    partner_flip,
    row_offset,
    col_offset,
    out,
    state,
    flux,
    above,
    low_cols,
    high_cols,
    wet,
    cover,
    placed,
    edges,
    row_send,
    row_recv,
    col_send,
    col_recv,
    up_send,
    up_recv,
    up_cross,
    down_cross_send,
    down_cross_recv,
    down_send,
    down_recv,
    load_sem,
    store_sem,
    send_sem,
    recv_sem,
):
    grid = lax.axis_index("grid")
    row = lax.axis_index("gx")
    col = lax.axis_index("gy")
    rows = lax.axis_size("gx")
    cols = lax.axis_size("gy")
    is_parent = grid == 0
    is_child = grid > 0
    partner = row + 1 - 2 * lax.rem(row, 2)
    slot_of = grid - 1
    sides = (
        (NORTH, row > 0, {"gx": row - 1}),
        (SOUTH, row < rows - 1, {"gx": row + 1}),
        (WEST, col > 0, {"gy": col - 1}),
        (EAST, col < cols - 1, {"gy": col + 1}),
    )

    loads = [
        pltpu.make_async_copy(
            adjoint.at[0, pl.ds(c * LEV, LEV), :, pl.ds(h * HC, HC)], state.at[:, c, h], load_sem.at[c, h]
        )
        for c in range(NCLS)
        for h in range(2)
    ]
    for load in loads:
        load.start()

    row_recv[...] = jnp.zeros_like(row_recv)
    col_recv[...] = jnp.zeros_like(col_recv)

    barrier = pltpu.get_barrier_semaphore()

    def greet(device):
        pl.semaphore_signal(barrier, inc=1, device_id=device, device_id_type=MESH)

    for _, there, device in sides:

        @pl.when(there)
        def _():
            greet(device)

    @pl.when(is_parent)
    def _():
        for slot in range(SLOTS):
            greet({"grid": slot + 1})

    @pl.when(is_child)
    def _():
        greet({"grid": 0})

    placed[...] = jnp.zeros_like(placed)
    wet[...] = sea_mask[0].astype(F32)

    def one(flag):
        return jnp.where(flag, 1, 0)

    tops = [row_offset[g, row, col] for g in range(SLOTS)] + [row_offset[g, partner, col] for g in range(SLOTS)]
    lefts = [col_offset[g, row, col] for g in range(SLOTS)] + [col_offset[g, partner, col] for g in range(SLOTS)]
    flags = [1 - partner_flip[g, row, col] for g in range(SLOTS)] + [partner_flip[g, partner, col] for g in range(SLOTS)]

    @pl.when(is_parent)
    def _():
        row_ids = iota((CR, CC), 0)
        col_ids = iota((CR, CC), 1)
        total = jnp.zeros((CR, CC), F32)
        for top, left, flag in zip(tops, lefts, flags):
            inside = (row_ids >= top) & (row_ids < top + HR) & (col_ids >= left) & (col_ids < left + HC)
            total = total + jnp.where(inside, flag.astype(F32), 0.0)
        cover[...] = 1.0 - relaxation * total

    pl.semaphore_wait(
        barrier,
        one(row > 0) + one(row < rows - 1) + one(col > 0) + one(col < cols - 1) + jnp.where(is_parent, SLOTS, 1),
    )
    for load in loads:
        load.wait()

    def copy(source, target, kind, trip, device, landing=None):
        return pltpu.make_async_remote_copy(
            src_ref=source,
            dst_ref=target,
            send_sem=send_sem.at[trip, kind],
            recv_sem=recv_sem.at[trip, kind if landing is None else landing],
            device_id=device,
            device_id_type=MESH,
        )

    def up_copy(trip):
        return copy(up_send.at[trip], up_recv.at[trip, slot_of], UP, trip, {"grid": 0}, UP + slot_of)

    def up_arrival(trip, slot):
        return copy(up_send.at[trip], up_recv.at[trip, slot], UP, trip, {"grid": slot + 1}, UP + slot)

    def up_cross_copy(trip):
        return copy(up_recv.at[trip], up_cross.at[trip], UP_X, trip, {"gx": partner})

    def down_cross_copy(trip):
        return copy(down_cross_send.at[trip], down_cross_recv.at[trip], DOWN_X, trip, {"gx": partner})

    def down_copy(trip, slot):
        return copy(down_send.at[trip, slot], down_recv.at[trip], DOWN + slot, trip, {"grid": slot + 1}, DOWN)

    def down_arrival(trip):
        return copy(down_send.at[trip, 0], down_recv.at[trip], DOWN, trip, {"grid": 0}, DOWN)

    def halo_copy(trip, side, device):
        if side < WEST:
            return copy(row_send.at[trip, side], row_recv.at[trip, 1 - side], side, trip, device, 1 - side)
        return copy(col_send.at[trip, side - WEST], col_recv.at[trip, EAST - side], side, trip, device, WEST + EAST - side)

    def halo_arrival(trip, side, device):
        if side < WEST:
            return copy(row_send.at[trip, side], row_recv.at[trip, side], side, trip, device, side)
        return copy(col_send.at[trip, side - WEST], col_recv.at[trip, side - WEST], side, trip, device, side)

    def base_level(chunk):
        return LEV - NL * (chunk + 1)

    def full(level, c):
        return jnp.concatenate([state[level, c, 0], state[level, c, 1]], axis=1)

    def put(level, c, values):
        state[level, c, 0] = values[:, :HC]
        state[level, c, 1] = values[:, HC:]

    def cut(level, c, top, left):
        shift = lax.rem(HC - left, HC)
        low = pltpu.roll(state[level, c, 0, pl.ds(top, HR), :], shift, 1)
        high = pltpu.roll(state[level, c, 1, pl.ds(top, HR), :], shift, 1)
        return jnp.where(iota((HR, HC), 1) < HC - left, low, high)

    def send_up(trip, chunk):
        base = base_level(chunk)
        weights = sponge[0]

        def component(level, c):
            product = weights * full(base + level, c)
            at = (level * NCLS + c) * CR
            low_cols[pl.ds(at, CR), :] = product[:, :HC]
            high_cols[pl.ds(at, CR), :] = product[:, HC:]

        @pl.loop(0, NL)
        def _(level):
            for c in range(NCLS):
                component(level, c)

        half = ROWS // 2
        low = low_cols[pl.ds(0, half, stride=2), :] + low_cols[pl.ds(1, half, stride=2), :]
        high = high_cols[pl.ds(0, half, stride=2), :] + high_cols[pl.ds(1, half, stride=2), :]
        selector = (iota((CC, HC), 0) // 2 == iota((CC, HC), 1)).astype(F32).astype(BF16)
        sums = exact_dot(jnp.concatenate([low, high], axis=1), selector)
        up_send[trip] = sums.reshape(NK, HR, HC)
        up_copy(trip).start()

    def send_cross(trip, chunk):
        base = base_level(chunk)

        @pl.loop(0, NL)
        def _(level):
            for c in range(NCLS):
                for slot in range(SLOTS):
                    down_cross_send[trip, slot, level * NCLS + c] = cut(
                        base + level, c, tops[SLOTS + slot], lefts[SLOTS + slot]
                    )

        down_cross_copy(trip).start()

    def send_down(trip, chunk):
        base = base_level(chunk)
        down_cross_copy(trip).wait_recv()
        for slot in range(SLOTS):
            keep = flags[slot].astype(F32)

            @pl.loop(0, NL)
            def _(level):
                for c in range(NCLS):
                    values = cut(base + level, c, tops[slot], lefts[slot])
                    other = down_cross_recv[trip, slot, level * NCLS + c]
                    down_send[trip, slot, level * NCLS + c] = keep * values + (1.0 - keep) * other

            down_copy(trip, slot).start()

    def forward_up(trip):
        for slot in range(SLOTS):
            up_arrival(trip, slot).wait_recv()
        up_cross_copy(trip).start()

    def nest_parent(trip, chunk):
        base = base_level(chunk)
        up_cross_copy(trip).wait_recv()
        lanes = iota((8, HC), 1)

        @pl.loop(0, NL)
        def _(level):
            for c in range(NCLS):
                k = level * NCLS + c
                old = full(base + level, c) * cover[...]
                low = old[:, :HC].reshape(CR // 8, 8, HC)
                high = old[:, HC:].reshape(CR // 8, 8, HC)
                for n in range(2 * SLOTS):
                    source = up_recv if n < SLOTS else up_cross
                    placed[c, n, HR : HR + HR] = source[trip, n % SLOTS, k]
                    piece = placed[c, n, pl.ds(HR - tops[n], CR), :]
                    piece = pltpu.roll(piece, lax.rem(lefts[n], HC), 1).reshape(CR // 8, 8, HC)
                    flag = flags[n].astype(F32)
                    low = low + jnp.where(lanes >= lefts[n], flag, 0.0)[None] * piece
                    high = high + jnp.where(lanes < lefts[n], flag, 0.0)[None] * piece
                state[base + level, c, 0] = low.reshape(CR, HC)
                state[base + level, c, 1] = high.reshape(CR, HC)

    def nest_child(trip, chunk):
        base = base_level(chunk)
        down_arrival(trip).wait_recv()
        selector = jnp.where(iota((HC, CC), 1) // 2 == iota((HC, CC), 0), relaxation / 4.0, 0.0).astype(BF16)
        half = ROWS // 2
        spread = exact_dot(down_recv[trip].reshape(NK * HR, HC), selector)
        for start in (0, 1):
            low_cols[pl.ds(start, half, stride=2), :] = spread[:, :HC]
            high_cols[pl.ds(start, half, stride=2), :] = spread[:, HC:]
        kept = 1.0 - sponge[0]

        @pl.loop(0, NL)
        def _(level):
            for c in range(NCLS):
                at = (level * NCLS + c) * CR
                added = jnp.concatenate([low_cols[pl.ds(at, CR), :], high_cols[pl.ds(at, CR), :]], axis=1)
                put(base + level, c, kept * full(base + level, c) + added)

    def local_part(trip, chunk):
        base = base_level(chunk)

        @pl.loop(0, NL)
        def _(index):
            level = NL - 1 - index
            u0 = full(base + level, 0)
            u1 = full(base + level, 1)
            u2 = full(base + level, 2)
            agg = aggregation[0]
            brk = breakup[0]
            flocced = (
                (1.0 - agg) * u0 + agg * u1,
                brk * u0 + (1.0 - agg - brk) * u1 + agg * u2,
                brk * u1 + (1.0 - brk) * u2,
            )
            for c in range(NCLS):
                rate = settling[grid, c]
                value = wet[...] * ((1.0 - rate) * flocced[c] + rate * above[c])
                above[c] = flocced[c]
                outward = diffusivity[0] * value
                k = level * NCLS + c
                put(base + level, c, value - 4.0 * outward)
                flux[trip, k, 8 : 8 + CR] = outward
                row_send[trip, 0, pl.ds(k, 1), :] = outward[0:1, :]
                row_send[trip, 1, pl.ds(k, 1), :] = outward[CR - 1 : CR, :]

        selector = jnp.where(iota((8, CC), 1) == iota((8, CC), 0) * (CC - 1), 1.0, 0.0).astype(BF16)
        high, low = halves(flux[trip, :, 8 : 8 + CR].reshape(ROWS, CC))
        dims = (((1,), (1,)), ((), ()))
        ends = lax.dot_general(selector, high, dims, preferred_element_type=F32) + lax.dot_general(
            selector, low, dims, preferred_element_type=F32
        )
        if WIDE > ROWS:
            ends = jnp.concatenate([ends, jnp.zeros((8, WIDE - ROWS), F32)], axis=1)
        col_send[trip, 0] = ends[0:1]
        col_send[trip, 1] = ends[1:2]
        for side, there, device in sides:

            @pl.when(there)
            def _():
                halo_copy(trip, side, device).start()

    def stencil(trip, chunk):
        base = base_level(chunk)
        for side, there, device in sides:

            @pl.when(there)
            def _():
                halo_arrival(trip, side, device).wait_recv()

        kind = iota((8, WIDE), 0)
        west = jnp.broadcast_to(col_recv[trip, 0], (8, WIDE))
        east = jnp.broadcast_to(col_recv[trip, 1], (8, WIDE))
        west_high = west.astype(BF16).astype(F32)
        east_high = east.astype(BF16).astype(F32)
        parts = jnp.where(
            kind == 0,
            west_high,
            jnp.where(kind == 1, west - west_high, jnp.where(kind == 2, east_high, jnp.where(kind == 3, east - east_high, 0.0))),
        )
        target = iota((8, CC), 0)
        lane = iota((8, CC), 1)
        selector = jnp.where(((target < 2) & (lane == 0)) | ((target >= 2) & (target < 4) & (lane == CC - 1)), 1.0, 0.0)
        edges[...] = jnp.dot(parts.T.astype(BF16), selector.astype(BF16), preferred_element_type=F32)

        @pl.loop(0, NL)
        def _(level):
            lane_ids = iota((CR, CC), 1)
            for c in range(NCLS):
                k = level * NCLS + c
                flux[trip, k, 7:8] = row_recv[trip, 0, pl.ds(k, 1), :]
                flux[trip, k, 8 + CR : 9 + CR] = row_recv[trip, 1, pl.ds(k, 1), :]
                middle = flux[trip, k, 8 : 8 + CR]
                left = jnp.where(lane_ids > 0, pltpu.roll(middle, 1, 1), 0.0)
                right = jnp.where(lane_ids < CC - 1, pltpu.roll(middle, CC - 1, 1), 0.0)
                put(
                    base + level,
                    c,
                    full(base + level, c)
                    + flux[trip, k, 7 : 7 + CR]
                    + flux[trip, k, 9 : 9 + CR]
                    + left
                    + right
                    + edges[pl.ds(k * CR, CR), :],
                )

    def first_sends(trip, chunk):
        @pl.when(is_parent)
        def _():
            send_cross(trip, chunk)

        @pl.when(is_child)
        def _():
            send_up(trip, chunk)

    def stores(chunk):
        base = base_level(chunk)
        return [
            pltpu.make_async_copy(
                state.at[pl.ds(base, NL), c, h],
                out.at[0, pl.ds(c * LEV + base, NL), :, pl.ds(h * HC, HC)],
                store_sem.at[chunk, c, h],
            )
            for c in range(NCLS)
            for h in range(2)
        ]

    @pl.loop(0, CHUNKS)
    def _(chunk):
        first_sends(chunk, chunk)

    for step in range(STEPS):
        start = step * CHUNKS

        @pl.when(is_parent)
        def _():
            @pl.loop(0, CHUNKS)
            def _(chunk):
                send_down(start + chunk, chunk)
                forward_up(start + chunk)

        above[...] = jnp.zeros_like(above)

        @pl.loop(0, CHUNKS)
        def _(chunk):
            @pl.when(is_parent)
            def _():
                nest_parent(start + chunk, chunk)

            @pl.when(is_child)
            def _():
                nest_child(start + chunk, chunk)

            local_part(start + chunk, chunk)

        @pl.loop(0, CHUNKS)
        def _(chunk):
            stencil(start + chunk, chunk)
            if step + 1 < STEPS:
                first_sends(start + CHUNKS + chunk, chunk)
            else:
                for store in stores(chunk):
                    store.start()

    @pl.loop(0, TRIPS)
    def _(trip):
        for side, there, device in sides:

            @pl.when(there)
            def _():
                halo_copy(trip, side, device).wait_send()

        @pl.when(is_parent)
        def _():
            down_cross_copy(trip).wait_send()
            up_cross_copy(trip).wait_send()
            for slot in range(SLOTS):
                down_copy(trip, slot).wait_send()

        @pl.when(is_child)
        def _():
            up_copy(trip).wait_send()

    @pl.loop(0, CHUNKS)
    def _(chunk):
        for store in stores(chunk):
            store.wait()


def local(*args):
    vmem = pl.BlockSpec(memory_space=pltpu.VMEM)
    smem = pl.BlockSpec(memory_space=pltpu.SMEM)
    hbm = pl.BlockSpec(memory_space=pl.ANY)
    return pl.pallas_call(
        kernel,
        out_shape=jax.ShapeDtypeStruct((1, NCLS * LEV, CR, CC), F32),
        in_specs=[hbm] + [vmem] * 5 + [smem] * 4,
        out_specs=hbm,
        scratch_shapes=[
            pltpu.VMEM((LEV, NCLS, 2, CR, HC), F32),
            pltpu.VMEM((TRIPS, NK, CR + 16, CC), F32),
            pltpu.VMEM((NCLS, CR, CC), F32),
            pltpu.VMEM((ROWS, HC), F32),
            pltpu.VMEM((ROWS, HC), F32),
            pltpu.VMEM((CR, CC), F32),
            pltpu.VMEM((CR, CC), F32),
            pltpu.VMEM((NCLS, 2 * SLOTS, 3 * HR, HC), F32),
            pltpu.VMEM((WIDE, CC), F32),
            pltpu.VMEM((TRIPS, 2, NKP, CC), F32),
            pltpu.VMEM((TRIPS, 2, NKP, CC), F32),
            pltpu.VMEM((TRIPS, 2, 1, WIDE), F32),
            pltpu.VMEM((TRIPS, 2, 1, WIDE), F32),
            pltpu.VMEM((TRIPS, NK, HR, HC), F32),
            pltpu.VMEM((TRIPS, SLOTS, NK, HR, HC), F32),
            pltpu.VMEM((TRIPS, SLOTS, NK, HR, HC), F32),
            pltpu.VMEM((TRIPS, SLOTS, NK, HR, HC), F32),
            pltpu.VMEM((TRIPS, SLOTS, NK, HR, HC), F32),
            pltpu.VMEM((TRIPS, SLOTS, NK, HR, HC), F32),
            pltpu.VMEM((TRIPS, NK, HR, HC), F32),
            pltpu.SemaphoreType.DMA((NCLS, 2)),
            pltpu.SemaphoreType.DMA((CHUNKS, NCLS, 2)),
            pltpu.SemaphoreType.DMA((TRIPS, KINDS)),
            pltpu.SemaphoreType.DMA((TRIPS, KINDS)),
        ],
        compiler_params=pltpu.CompilerParams(
            collective_id=0, has_side_effects=True, vmem_limit_bytes=40 * 1024 * 1024
        ),
        name="nested_steps",
    )(*args)


def solution(mesh):
    tile = P("grid", "gx", "gy")
    in_specs = (P("grid", None, "gx", "gy"),) + (tile,) * 5 + (P(),) * 4
    return jax.shard_map(
        local, mesh=mesh, in_specs=in_specs, out_specs=P("grid", None, "gx", "gy"), check_vma=False
    )
```

```python
import functools

import jax
import jax.numpy as jnp
from jax import lax
from jax.experimental import pallas as pl
from jax.experimental.pallas import tpu as pltpu
from jax.sharding import PartitionSpec as P

NCLS = 3
LEV = 8
STEPS = 2
CR = 32
CC = 256
HR = 16
HC = 128
SLOTS = 3
relaxation = 0.125

CHUNKS = 8
NL = LEV // CHUNKS
NK = NL * NCLS
NKP = -(-NK // 8) * 8
ROWS = NK * CR
WIDE = NL * HC
TRIPS = STEPS * CHUNKS
MESH = pl.DeviceIdType.MESH
F32 = jnp.float32
BF16 = jnp.bfloat16

NORTH, SOUTH, WEST, EAST, UP, UP_X, RELAY, DOWN_X, DOWN = 0, 1, 2, 3, 4, 7, 8, 9, 10
KINDS = 11
LAG = 3
LEAD_SEND, LEAD_ANSWER, LEAD_RELAY = CHUNKS - LAG, 2, 4


def iota(shape, dim):
    return lax.broadcasted_iota(jnp.int32, shape, dim)


def halves(x):
    high = x.astype(BF16)
    return high, (x - high.astype(F32)).astype(BF16)


def exact_dot(x, selector):
    high, low = halves(x)
    return jnp.dot(high, selector, preferred_element_type=F32) + jnp.dot(low, selector, preferred_element_type=F32)


def kernel(
    adjoint,
    sea_mask_in,
    diffusivity_in,
    aggregation_in,
    breakup_in,
    sponge_in,
    settling_in,
    partner_flip_in,
    row_offset_in,
    col_offset_in,
    out,
    sea_mask,
    diffusivity,
    aggregation,
    breakup,
    sponge,
    settling,
    partner_flip,
    row_offset,
    col_offset,
    state,
    flux,
    above,
    low_cols,
    high_cols,
    wet,
    cover,
    placed,
    row_send,
    row_recv,
    col_send,
    col_recv,
    up_send,
    up_recv,
    relayed,
    up_cross,
    down_cross_send,
    down_cross_recv,
    down_send,
    down_recv,
    field_sem,
    load_sem,
    store_sem,
    send_sem,
    recv_sem,
):
    grid = lax.axis_index("grid")
    row = lax.axis_index("gx")
    col = lax.axis_index("gy")
    rows = lax.axis_size("gx")
    cols = lax.axis_size("gy")
    is_parent = grid == 0
    is_child = grid > 0
    is_relay = grid == SLOTS
    behind = lax.rem(col + cols - 2, cols)
    ahead = lax.rem(col + 2, cols)
    partner = row + 1 - 2 * lax.rem(row, 2)
    slot_of = grid - 1
    sides = (
        (NORTH, {"gx": lax.rem(row + rows - 1, rows)}),
        (SOUTH, {"gx": lax.rem(row + 1, rows)}),
        (WEST, {"gy": lax.rem(col + cols - 1, cols)}),
        (EAST, {"gy": lax.rem(col + 1, cols)}),
    )
    inner = [
        jnp.where(joint, 0.0, 1.0) for joint in (row == 0, row == rows - 1, col == 0, col == cols - 1)
    ]

    fields = [
        pltpu.make_async_copy(source, target, field_sem.at[n])
        for n, (source, target) in enumerate(
            (
                (partner_flip_in, partner_flip),
                (row_offset_in, row_offset),
                (col_offset_in, col_offset),
                (settling_in, settling),
                (sponge_in, sponge),
                (sea_mask_in, sea_mask),
                (diffusivity_in, diffusivity),
                (aggregation_in, aggregation),
                (breakup_in, breakup),
            )
        )
    ]
    loads = [
        pltpu.make_async_copy(
            adjoint.at[0, pl.ds(c * LEV, LEV), :, pl.ds(h * HC, HC)], state.at[:, c, h], load_sem.at[c, h]
        )
        for c in range(NCLS)
        for h in range(2)
    ]
    for load in fields[:3] + loads + fields[3:]:
        load.start()

    barrier = pltpu.get_barrier_semaphore()

    def greet(device):
        pl.semaphore_signal(barrier, inc=1, device_id=device, device_id_type=MESH)

    for _, device in sides:
        greet(device)

    @pl.when(is_parent)
    def _():
        for slot in range(SLOTS):
            greet({"grid": slot + 1})
        greet({"grid": SLOTS, "gx": partner, "gy": behind})
        greet({"grid": SLOTS, "gy": behind})

    @pl.when(is_child)
    def _():
        greet({"grid": 0})

    @pl.when(is_relay)
    def _():
        greet({"grid": 0, "gx": partner, "gy": ahead})
        greet({"grid": 0, "gy": ahead})

    placed[...] = jnp.zeros_like(placed)
    for load in fields:
        load.wait()
    wet[...] = sea_mask[0].astype(F32)

    tops = [row_offset[g, col, row] for g in range(SLOTS)] + [row_offset[g, col, partner] for g in range(SLOTS)]
    lefts = [col_offset[g, col, row] for g in range(SLOTS)] + [col_offset[g, col, partner] for g in range(SLOTS)]
    flags = [1 - partner_flip[g, col, row] for g in range(SLOTS)] + [partner_flip[g, col, partner] for g in range(SLOTS)]

    @pl.when(is_parent)
    def _():
        row_ids = iota((CR, CC), 0)
        col_ids = iota((CR, CC), 1)
        total = jnp.zeros((CR, CC), F32)
        for top, left, flag in zip(tops, lefts, flags):
            inside = (row_ids >= top) & (row_ids < top + HR) & (col_ids >= left) & (col_ids < left + HC)
            total = total + jnp.where(inside, flag.astype(F32), 0.0)
        cover[...] = 1.0 - relaxation * total

    pl.semaphore_wait(
        barrier,
        4 + jnp.where(is_parent, SLOTS + 2, 1) + jnp.where(is_relay, 2, 0),
    )
    for load in loads:
        load.wait()

    def copy(source, target, kind, trip, device, landing=None):
        return pltpu.make_async_remote_copy(
            src_ref=source,
            dst_ref=target,
            send_sem=send_sem.at[kind],
            recv_sem=recv_sem.at[trip, kind if landing is None else landing],
            device_id=device,
            device_id_type=MESH,
        )

    def up_copy(trip):
        return copy(up_send.at[trip], up_recv.at[trip, slot_of], UP, trip, {"grid": 0}, UP + slot_of)

    def up_arrival(trip, slot):
        return copy(up_send.at[trip], up_recv.at[trip, slot], UP, trip, {"grid": slot + 1}, UP + slot)

    def up_cross_copy(trip):
        return copy(up_recv.at[trip], up_cross.at[trip], UP_X, trip, {"gx": partner})

    def relay_copy(trip):
        return copy(
            down_cross_send.at[trip], relayed.at[trip], RELAY, trip, {"grid": SLOTS, "gx": partner, "gy": behind}
        )

    def down_cross_copy(trip):
        return copy(relayed.at[trip], down_cross_recv.at[trip], DOWN_X, trip, {"grid": 0, "gy": ahead})

    def down_copy(trip, slot):
        return copy(down_send.at[trip, slot], down_recv.at[trip], DOWN, trip, {"grid": slot + 1})

    def down_arrival(trip):
        return copy(down_send.at[trip, 0], down_recv.at[trip], DOWN, trip, {"grid": 0}, DOWN)

    def halo_copy(trip, side, device):
        if side < WEST:
            return copy(row_send.at[trip, side], row_recv.at[trip, 1 - side], side, trip, device, 1 - side)
        return copy(col_send.at[trip, side - WEST], col_recv.at[trip, EAST - side], side, trip, device, WEST + EAST - side)

    def halo_arrival(trip, side, device):
        if side < WEST:
            return copy(row_send.at[trip, side], row_recv.at[trip, side], side, trip, device, side)
        return copy(col_send.at[trip, side - WEST], col_recv.at[trip, side - WEST], side, trip, device, side)

    def base_level(chunk):
        return LEV - NL * (chunk + 1)

    def full(level, c):
        return jnp.concatenate([state[level, c, 0], state[level, c, 1]], axis=1)

    def put(level, c, values):
        state[level, c, 0] = values[:, :HC]
        state[level, c, 1] = values[:, HC:]

    def cut(level, c, top, left):
        low = state[level, c, 0, pl.ds(top, HR), :]
        high = state[level, c, 1, pl.ds(top, HR), :]
        return pltpu.roll(jnp.where(iota((HR, HC), 1) >= left, low, high), lax.rem(HC - left, HC), 1)

    def send_up(trip, chunk):
        base = base_level(chunk)
        weights = sponge[0]

        def component(level, c):
            product = weights * full(base + level, c)
            at = (level * NCLS + c) * CR
            low_cols[pl.ds(at, CR), :] = product[:, :HC]
            high_cols[pl.ds(at, CR), :] = product[:, HC:]

        for level in range(NL):
            for c in range(NCLS):
                component(level, c)

        half = ROWS // 2
        low = low_cols[pl.ds(0, half, stride=2), :] + low_cols[pl.ds(1, half, stride=2), :]
        high = high_cols[pl.ds(0, half, stride=2), :] + high_cols[pl.ds(1, half, stride=2), :]
        selector = (iota((CC, HC), 0) // 2 == iota((CC, HC), 1)).astype(F32).astype(BF16)
        sums = exact_dot(jnp.concatenate([low, high], axis=1), selector)
        up_send[trip] = sums.reshape(NK, HR, HC)
        up_copy(trip).start()

    def send_cross(trip, chunk):
        base = base_level(chunk)

        for level in range(NL):
            for c in range(NCLS):
                for slot in range(SLOTS):
                    down_cross_send[trip, slot, level * NCLS + c] = cut(
                        base + level, c, tops[SLOTS + slot], lefts[SLOTS + slot]
                    )

        relay_copy(trip).start()

    def send_down(trip, chunk):
        base = base_level(chunk)
        down_cross_copy(trip).wait_recv()
        for slot in range(SLOTS):
            keep = flags[slot].astype(F32)

            for level in range(NL):
                for c in range(NCLS):
                    values = cut(base + level, c, tops[slot], lefts[slot])
                    other = down_cross_recv[trip, slot, level * NCLS + c]
                    down_send[trip, slot, level * NCLS + c] = keep * values + (1.0 - keep) * other

            down_copy(trip, slot).start()

    def forward_up(trip):
        for slot in range(SLOTS):
            up_arrival(trip, slot).wait_recv()
        up_cross_copy(trip).start()

    def relay(trip):
        relay_copy(trip).wait_recv()
        down_cross_copy(trip).start()

    def nest_parent(trip, chunk):
        base = base_level(chunk)
        up_cross_copy(trip).wait_recv()
        lanes = iota((8, HC), 1)

        for level in range(NL):
            for c in range(NCLS):
                k = level * NCLS + c
                old = full(base + level, c) * cover[...]
                low = old[:, :HC].reshape(CR // 8, 8, HC)
                high = old[:, HC:].reshape(CR // 8, 8, HC)
                for n in range(2 * SLOTS):
                    source = up_recv if n < SLOTS else up_cross
                    placed[c, n, HR : HR + HR] = pltpu.roll(source[trip, n % SLOTS, k], lax.rem(lefts[n], HC), 1)
                    piece = placed[c, n, pl.ds(HR - tops[n], CR), :].reshape(CR // 8, 8, HC)
                    flag = flags[n].astype(F32)
                    low = low + jnp.where(lanes >= lefts[n], flag, 0.0)[None] * piece
                    high = high + jnp.where(lanes < lefts[n], flag, 0.0)[None] * piece
                state[base + level, c, 0] = low.reshape(CR, HC)
                state[base + level, c, 1] = high.reshape(CR, HC)

    def nest_child(trip, chunk):
        base = base_level(chunk)
        down_arrival(trip).wait_recv()
        selector = jnp.where(iota((HC, CC), 1) // 2 == iota((HC, CC), 0), relaxation / 4.0, 0.0).astype(BF16)
        half = ROWS // 2
        spread = exact_dot(down_recv[trip].reshape(NK * HR, HC), selector)
        for start in (0, 1):
            low_cols[pl.ds(start, half, stride=2), :] = spread[:, :HC]
            high_cols[pl.ds(start, half, stride=2), :] = spread[:, HC:]
        kept = 1.0 - sponge[0]

        for level in range(NL):
            for c in range(NCLS):
                at = (level * NCLS + c) * CR
                added = jnp.concatenate([low_cols[pl.ds(at, CR), :], high_cols[pl.ds(at, CR), :]], axis=1)
                put(base + level, c, kept * full(base + level, c) + added)

    def local_part(trip, chunk):
        base = base_level(chunk)

        @pl.when(chunk == 0)
        def _():
            above[...] = jnp.zeros_like(above)

        for level in reversed(range(NL)):
            u0 = full(base + level, 0)
            u1 = full(base + level, 1)
            u2 = full(base + level, 2)
            agg = aggregation[0]
            brk = breakup[0]
            flocced = (
                (1.0 - agg) * u0 + agg * u1,
                brk * u0 + (1.0 - agg - brk) * u1 + agg * u2,
                brk * u1 + (1.0 - brk) * u2,
            )
            columns = []
            for c in range(NCLS):
                rate = settling[grid, c]
                value = wet[...] * ((1.0 - rate) * flocced[c] + rate * above[c])
                above[c] = flocced[c]
                outward = diffusivity[0] * value
                k = level * NCLS + c
                put(base + level, c, value - 4.0 * outward)
                flux[trip, k, 8 : 8 + CR] = outward
                row_send[trip, 0, pl.ds(k, 1), :] = outward[0:1, :]
                row_send[trip, 1, pl.ds(k, 1), :] = outward[CR - 1 : CR, :]
                columns.append(jnp.where(iota((CR, HC), 1) < HC // 2, outward[:, :HC], outward[:, HC:]))

            square = jnp.concatenate(columns + [jnp.zeros((HC - NCLS * CR, HC), F32)], axis=0).T
            col_send[trip, 0, :, level * HC : (level + 1) * HC] = square[0:1]
            col_send[trip, 1, :, level * HC : (level + 1) * HC] = square[HC - 1 : HC]


        for side, device in sides:
            halo_copy(trip, side, device).start()

    def stencil(trip, chunk):
        base = base_level(chunk)
        for side, device in sides:
            halo_arrival(trip, side, device).wait_recv()

        for level in range(NL):
            for c in range(NCLS):
                k = level * NCLS + c
                flux[trip, k, 7:8] = inner[NORTH] * row_recv[trip, 0, pl.ds(k, 1), :]
                flux[trip, k, 8 + CR : 9 + CR] = inner[SOUTH] * row_recv[trip, 1, pl.ds(k, 1), :]
            west = inner[WEST] * col_recv[trip, 0, :, level * HC : (level + 1) * HC]
            east = inner[EAST] * col_recv[trip, 1, :, level * HC : (level + 1) * HC]
            kind = iota((HC, HC), 0)
            square = jnp.where(kind == 0, west, jnp.where(kind == HC - 1, east, 0.0)).T
            lanes = iota((CR, HC), 1)
            lane_ids = iota((CR, CC), 1)
            results = []
            for c in range(NCLS):
                k = level * NCLS + c
                middle = flux[trip, k, 8 : 8 + CR]
                left = jnp.where(lane_ids > 0, pltpu.roll(middle, 1, 1), 0.0)
                right = jnp.where(lane_ids < CC - 1, pltpu.roll(middle, CC - 1, 1), 0.0)
                ends = square[c * CR : (c + 1) * CR]
                ends = jnp.concatenate(
                    [jnp.where(lanes < HC // 2, ends, 0.0), jnp.where(lanes >= HC // 2, ends, 0.0)], axis=1
                )
                results.append(
                    full(base + level, c)
                    + flux[trip, k, 7 : 7 + CR]
                    + flux[trip, k, 9 : 9 + CR]
                    + left
                    + right
                    + ends
                )
            for c in range(NCLS):
                put(base + level, c, results[c])

    def first_sends(trip, chunk):
        @pl.when(is_parent)
        def _():
            send_cross(trip, chunk)

        @pl.when(is_child)
        def _():
            send_up(trip, chunk)

    def stores(chunk):
        base = base_level(chunk)
        return [
            pltpu.make_async_copy(
                state.at[base + level, :, h],
                out.at[0, :, base + level, :, pl.ds(h * HC, HC)],
                store_sem.at[chunk, level, h],
            )
            for level in range(NL)
            for h in range(2)
        ]

    def in_range(trip):
        return (trip >= 0) & (trip < TRIPS)

    @pl.loop(0, TRIPS + LEAD_SEND + LAG)
    def _(tick):
        now = tick - LEAD_SEND

        @pl.when(now >= LAG)
        def _():
            stencil(now - LAG, lax.rem(now - LAG + CHUNKS, CHUNKS))

        @pl.when(now >= CHUNKS + LAG)
        def _():
            for store in stores(now - LAG - CHUNKS):
                store.start()

        sending = now + LEAD_SEND

        @pl.when(sending < TRIPS)
        def _():
            first_sends(sending, lax.rem(sending, CHUNKS))

        answering = now + LEAD_ANSWER

        @pl.when(is_parent & in_range(answering))
        def _():
            send_down(answering, lax.rem(answering + CHUNKS, CHUNKS))
            forward_up(answering)

        relaying = now + LEAD_RELAY

        @pl.when(is_relay & in_range(relaying))
        def _():
            relay(relaying)

        @pl.when(in_range(now))
        def _():
            chunk = lax.rem(now + CHUNKS, CHUNKS)

            @pl.when(is_parent)
            def _():
                nest_parent(now, chunk)

            @pl.when(is_child)
            def _():
                nest_child(now, chunk)

            local_part(now, chunk)

    def sent(source, kind, device):
        copy(source, source, kind, 0, device).wait_send()

    for side, device in sides:
        sent(row_send.at[:, side] if side < WEST else col_send.at[:, side - WEST], side, device)

    @pl.when(is_parent)
    def _():
        sent(down_cross_send, RELAY, {"gx": partner})
        sent(up_recv, UP_X, {"gx": partner})
        sent(down_send, DOWN, {"gx": partner})

    @pl.when(is_child)
    def _():
        sent(up_send, UP, {"grid": 0})

    @pl.when(is_relay)
    def _():
        sent(relayed, DOWN_X, {"grid": 0})

    @pl.loop(0, CHUNKS)
    def _(chunk):
        for store in stores(chunk):
            store.wait()


def local(adjoint, sea_mask, diffusivity, aggregation, breakup, sponge, settling, *tables):
    hbm = pl.BlockSpec(memory_space=pl.ANY)
    return pl.pallas_call(
        kernel,
        out_shape=jax.ShapeDtypeStruct((1, NCLS, LEV, CR, CC), F32),
        in_specs=[hbm] * 10,
        out_specs=hbm,
        scratch_shapes=[
            pltpu.VMEM((1, CR, CC), jnp.int32),
            pltpu.VMEM((1, CR, CC), F32),
            pltpu.VMEM((1, CR, CC), F32),
            pltpu.VMEM((1, CR, CC), F32),
            pltpu.VMEM((1, CR, CC), F32),
            pltpu.SMEM(settling.shape, F32),
        ]
        + [pltpu.SMEM((t.shape[0], t.shape[2], t.shape[1]), jnp.int32) for t in tables]
        + [
            pltpu.VMEM((LEV, NCLS, 2, CR, HC), F32),
            pltpu.VMEM((TRIPS, NK, CR + 16, CC), F32),
            pltpu.VMEM((NCLS, CR, CC), F32),
            pltpu.VMEM((ROWS, HC), F32),
            pltpu.VMEM((ROWS, HC), F32),
            pltpu.VMEM((CR, CC), F32),
            pltpu.VMEM((CR, CC), F32),
            pltpu.VMEM((NCLS, 2 * SLOTS, 3 * HR, HC), F32),
            pltpu.VMEM((TRIPS, 2, NKP, CC), F32),
            pltpu.VMEM((TRIPS, 2, NKP, CC), F32),
            pltpu.VMEM((TRIPS, 2, 1, WIDE), F32),
            pltpu.VMEM((TRIPS, 2, 1, WIDE), F32),
            pltpu.VMEM((TRIPS, NK, HR, HC), F32),
            pltpu.VMEM((TRIPS, SLOTS, NK, HR, HC), F32),
            pltpu.VMEM((TRIPS, SLOTS, NK, HR, HC), F32),
            pltpu.VMEM((TRIPS, SLOTS, NK, HR, HC), F32),
            pltpu.VMEM((TRIPS, SLOTS, NK, HR, HC), F32),
            pltpu.VMEM((TRIPS, SLOTS, NK, HR, HC), F32),
            pltpu.VMEM((TRIPS, SLOTS, NK, HR, HC), F32),
            pltpu.VMEM((TRIPS, NK, HR, HC), F32),
            pltpu.SemaphoreType.DMA((9,)),
            pltpu.SemaphoreType.DMA((NCLS, 2)),
            pltpu.SemaphoreType.DMA((CHUNKS, NL, 2)),
            pltpu.SemaphoreType.DMA((KINDS,)),
            pltpu.SemaphoreType.DMA((TRIPS, KINDS)),
        ],
        compiler_params=pltpu.CompilerParams(
            collective_id=0, has_side_effects=True, vmem_limit_bytes=60 * 1024 * 1024
        ),
        name="nested_steps",
    )(
        adjoint,
        sea_mask,
        diffusivity,
        aggregation,
        breakup,
        sponge,
        settling,
        *(t.transpose(0, 2, 1) for t in tables),
    ).reshape(1, NCLS * LEV, CR, CC)


def solution(mesh):
    tile = P("grid", "gx", "gy")
    in_specs = (P("grid", None, "gx", "gy"),) + (tile,) * 5 + (P(),) * 4
    return jax.shard_map(
        local, mesh=mesh, in_specs=in_specs, out_specs=P("grid", None, "gx", "gy"), check_vma=False
    )
```

```python
import functools

import jax
import jax.numpy as jnp
from jax import lax
from jax.experimental import pallas as pl
from jax.experimental.pallas import tpu as pltpu
from jax.sharding import PartitionSpec as P

NCLS = 3
LEV = 8
STEPS = 2
CR = 32
CC = 256
HR = 16
HC = 128
SLOTS = 3
relaxation = 0.125

CHUNKS = 8
NL = LEV // CHUNKS
NK = NL * NCLS
NKP = -(-NK // 8) * 8
ROWS = NK * CR
WIDE = NL * HC
TRIPS = STEPS * CHUNKS
MESH = pl.DeviceIdType.MESH
F32 = jnp.float32
BF16 = jnp.bfloat16

NORTH, SOUTH, WEST, EAST, UP, UP_X, RELAY, DOWN_X, DOWN = 0, 1, 2, 3, 4, 7, 8, 9, 10
KINDS = 11
SHORT, SHORT_END = 2, 8
SHORTS = SHORT * (SHORT_END // CHUNKS)
LAG = 2
LEAD_SEND, LEAD_ANSWER, LEAD_RELAY = CHUNKS - LAG, 2, 4


def iota(shape, dim):
    return lax.broadcasted_iota(jnp.int32, shape, dim)


def halves(x):
    high = x.astype(BF16)
    return high, (x - high.astype(F32)).astype(BF16)


def exact_dot(x, selector):
    high, low = halves(x)
    return jnp.dot(high, selector, preferred_element_type=F32) + jnp.dot(low, selector, preferred_element_type=F32)


def kernel(
    adjoint,
    sea_mask_in,
    diffusivity_in,
    aggregation_in,
    breakup_in,
    sponge_in,
    settling_in,
    partner_flip_in,
    row_offset_in,
    col_offset_in,
    out,
    sea_mask,
    diffusivity,
    aggregation,
    breakup,
    sponge,
    settling,
    partner_flip,
    row_offset,
    col_offset,
    state,
    flux,
    above,
    low_cols,
    high_cols,
    wet,
    cover,
    placed,
    row_send,
    row_recv,
    col_send,
    col_recv,
    up_send,
    up_recv,
    relayed,
    up_cross,
    down_cross_send,
    down_cross_recv,
    down_send,
    down_recv,
    field_sem,
    load_sem,
    store_sem,
    send_sem,
    recv_sem,
):
    grid = lax.axis_index("grid")
    row = lax.axis_index("gx")
    col = lax.axis_index("gy")
    rows = lax.axis_size("gx")
    cols = lax.axis_size("gy")
    is_parent = grid == 0
    is_child = grid > 0
    is_relay = grid == SLOTS
    behind = lax.rem(col + cols - 2, cols)
    ahead = lax.rem(col + 2, cols)
    partner = row + 1 - 2 * lax.rem(row, 2)
    slot_of = grid - 1
    sides = (
        (NORTH, {"gx": lax.rem(row + rows - 1, rows)}),
        (SOUTH, {"gx": lax.rem(row + 1, rows)}),
        (WEST, {"gy": lax.rem(col + cols - 1, cols)}),
        (EAST, {"gy": lax.rem(col + 1, cols)}),
    )
    inner = [
        jnp.where(joint, 0.0, 1.0) for joint in (row == 0, row == rows - 1, col == 0, col == cols - 1)
    ]

    fields = [
        pltpu.make_async_copy(source, target, field_sem.at[n])
        for n, (source, target) in enumerate(
            (
                (partner_flip_in, partner_flip),
                (row_offset_in, row_offset),
                (col_offset_in, col_offset),
                (settling_in, settling),
                (sponge_in, sponge),
                (sea_mask_in, sea_mask),
                (diffusivity_in, diffusivity),
                (aggregation_in, aggregation),
                (breakup_in, breakup),
            )
        )
    ]
    loads = [
        pltpu.make_async_copy(
            adjoint.at[0, pl.ds(c * LEV, LEV), :, pl.ds(h * HC, HC)], state.at[:, c, h], load_sem.at[c, h]
        )
        for c in range(NCLS)
        for h in range(2)
    ]
    for load in fields[:3] + loads + fields[3:]:
        load.start()

    barrier = pltpu.get_barrier_semaphore()

    def greet(device):
        pl.semaphore_signal(barrier, inc=1, device_id=device, device_id_type=MESH)

    for _, device in sides:
        greet(device)

    @pl.when(is_parent)
    def _():
        for slot in range(SLOTS):
            greet({"grid": slot + 1})
        greet({"grid": SLOTS, "gx": partner, "gy": behind})
        greet({"grid": SLOTS, "gy": behind})

    @pl.when(is_child)
    def _():
        greet({"grid": 0})

    @pl.when(is_relay)
    def _():
        greet({"grid": 0, "gx": partner, "gy": ahead})
        greet({"grid": 0, "gy": ahead})

    placed[...] = jnp.zeros_like(placed)
    for load in fields:
        load.wait()
    wet[...] = sea_mask[0].astype(F32)

    tops = [row_offset[g, col, row] for g in range(SLOTS)] + [row_offset[g, col, partner] for g in range(SLOTS)]
    lefts = [col_offset[g, col, row] for g in range(SLOTS)] + [col_offset[g, col, partner] for g in range(SLOTS)]
    flags = [1 - partner_flip[g, col, row] for g in range(SLOTS)] + [partner_flip[g, col, partner] for g in range(SLOTS)]

    @pl.when(is_parent)
    def _():
        row_ids = iota((CR, CC), 0)
        col_ids = iota((CR, CC), 1)
        total = jnp.zeros((CR, CC), F32)
        for top, left, flag in zip(tops, lefts, flags):
            inside = (row_ids >= top) & (row_ids < top + HR) & (col_ids >= left) & (col_ids < left + HC)
            total = total + jnp.where(inside, flag.astype(F32), 0.0)
        cover[...] = 1.0 - relaxation * total

    pl.semaphore_wait(
        barrier,
        4 + jnp.where(is_parent, SLOTS + 2, 1) + jnp.where(is_relay, 2, 0),
    )
    for load in loads:
        load.wait()

    def copy(source, target, kind, trip, device, landing=None):
        return pltpu.make_async_remote_copy(
            src_ref=source,
            dst_ref=target,
            send_sem=send_sem.at[kind],
            recv_sem=recv_sem.at[trip, kind if landing is None else landing],
            device_id=device,
            device_id_type=MESH,
        )

    def up_copy(trip):
        return copy(up_send.at[trip], up_recv.at[trip, slot_of], UP, trip, {"grid": 0}, UP + slot_of)

    def up_arrival(trip, slot):
        return copy(up_send.at[trip], up_recv.at[trip, slot], UP, trip, {"grid": slot + 1}, UP + slot)

    def up_cross_copy(trip):
        return copy(up_recv.at[trip], up_cross.at[trip], UP_X, trip, {"gx": partner})

    def relay_copy(trip):
        return copy(
            down_cross_send.at[trip], relayed.at[trip], RELAY, trip, {"grid": SLOTS, "gx": partner, "gy": behind}
        )

    def short(trip):
        return (lax.rem(trip, CHUNKS) < SHORT) & (trip < SHORT_END)

    def direct_copy(trip):
        return copy(
            down_cross_send.at[trip], down_cross_recv.at[trip], RELAY, trip, {"gx": partner}, DOWN_X
        )

    def down_cross_copy(trip):
        return copy(relayed.at[trip], down_cross_recv.at[trip], DOWN_X, trip, {"grid": 0, "gy": ahead})

    def down_copy(trip, slot):
        return copy(down_send.at[trip, slot], down_recv.at[trip], DOWN, trip, {"grid": slot + 1})

    def down_arrival(trip):
        return copy(down_send.at[trip, 0], down_recv.at[trip], DOWN, trip, {"grid": 0}, DOWN)

    def halo_copy(trip, side, device):
        if side < WEST:
            return copy(row_send.at[trip, side], row_recv.at[trip, 1 - side], side, trip, device, 1 - side)
        return copy(col_send.at[trip, side - WEST], col_recv.at[trip, EAST - side], side, trip, device, WEST + EAST - side)

    def halo_arrival(trip, side, device):
        if side < WEST:
            return copy(row_send.at[trip, side], row_recv.at[trip, side], side, trip, device, side)
        return copy(col_send.at[trip, side - WEST], col_recv.at[trip, side - WEST], side, trip, device, side)

    def base_level(chunk):
        return LEV - NL * (chunk + 1)

    def full(level, c):
        return jnp.concatenate([state[level, c, 0], state[level, c, 1]], axis=1)

    def put(level, c, values):
        state[level, c, 0] = values[:, :HC]
        state[level, c, 1] = values[:, HC:]

    def cut(level, c, top, left):
        low = state[level, c, 0, pl.ds(top, HR), :]
        high = state[level, c, 1, pl.ds(top, HR), :]
        return pltpu.roll(jnp.where(iota((HR, HC), 1) >= left, low, high), lax.rem(HC - left, HC), 1)

    def send_up(trip, chunk):
        base = base_level(chunk)
        weights = sponge[0]

        def component(level, c):
            product = weights * full(base + level, c)
            at = (level * NCLS + c) * CR
            low_cols[pl.ds(at, CR), :] = product[:, :HC]
            high_cols[pl.ds(at, CR), :] = product[:, HC:]

        for level in range(NL):
            for c in range(NCLS):
                component(level, c)

        half = ROWS // 2
        low = low_cols[pl.ds(0, half, stride=2), :] + low_cols[pl.ds(1, half, stride=2), :]
        high = high_cols[pl.ds(0, half, stride=2), :] + high_cols[pl.ds(1, half, stride=2), :]
        selector = (iota((CC, HC), 0) // 2 == iota((CC, HC), 1)).astype(F32).astype(BF16)
        sums = exact_dot(jnp.concatenate([low, high], axis=1), selector)
        up_send[trip] = sums.reshape(NK, HR, HC)
        up_copy(trip).start()

    def send_cross(trip, chunk):
        base = base_level(chunk)

        for level in range(NL):
            for c in range(NCLS):
                for slot in range(SLOTS):
                    down_cross_send[trip, slot, level * NCLS + c] = cut(
                        base + level, c, tops[SLOTS + slot], lefts[SLOTS + slot]
                    )

        @pl.when(short(trip))
        def _():
            direct_copy(trip).start()

        @pl.when(jnp.logical_not(short(trip)))
        def _():
            relay_copy(trip).start()

    def send_down(trip, chunk):
        base = base_level(chunk)
        down_cross_copy(trip).wait_recv()
        for slot in range(SLOTS):
            keep = flags[slot].astype(F32)

            for level in range(NL):
                for c in range(NCLS):
                    values = cut(base + level, c, tops[slot], lefts[slot])
                    other = down_cross_recv[trip, slot, level * NCLS + c]
                    down_send[trip, slot, level * NCLS + c] = keep * values + (1.0 - keep) * other

            down_copy(trip, slot).start()

    def forward_up(trip):
        for slot in range(SLOTS):
            up_arrival(trip, slot).wait_recv()
        up_cross_copy(trip).start()

    def relay(trip):
        relay_copy(trip).wait_recv()
        down_cross_copy(trip).start()

    def nest_parent(trip, chunk):
        base = base_level(chunk)
        up_cross_copy(trip).wait_recv()
        lanes = iota((8, HC), 1)

        for level in range(NL):
            for c in range(NCLS):
                k = level * NCLS + c
                old = full(base + level, c) * cover[...]
                low = old[:, :HC].reshape(CR // 8, 8, HC)
                high = old[:, HC:].reshape(CR // 8, 8, HC)
                for n in range(2 * SLOTS):
                    source = up_recv if n < SLOTS else up_cross
                    placed[c, n, HR : HR + HR] = pltpu.roll(source[trip, n % SLOTS, k], lax.rem(lefts[n], HC), 1)
                    piece = placed[c, n, pl.ds(HR - tops[n], CR), :].reshape(CR // 8, 8, HC)
                    flag = flags[n].astype(F32)
                    low = low + jnp.where(lanes >= lefts[n], flag, 0.0)[None] * piece
                    high = high + jnp.where(lanes < lefts[n], flag, 0.0)[None] * piece
                state[base + level, c, 0] = low.reshape(CR, HC)
                state[base + level, c, 1] = high.reshape(CR, HC)

    def nest_child(trip, chunk):
        base = base_level(chunk)
        down_arrival(trip).wait_recv()
        selector = jnp.where(iota((HC, CC), 1) // 2 == iota((HC, CC), 0), relaxation / 4.0, 0.0).astype(BF16)
        half = ROWS // 2
        spread = exact_dot(down_recv[trip].reshape(NK * HR, HC), selector)
        for start in (0, 1):
            low_cols[pl.ds(start, half, stride=2), :] = spread[:, :HC]
            high_cols[pl.ds(start, half, stride=2), :] = spread[:, HC:]
        kept = 1.0 - sponge[0]

        for level in range(NL):
            for c in range(NCLS):
                at = (level * NCLS + c) * CR
                added = jnp.concatenate([low_cols[pl.ds(at, CR), :], high_cols[pl.ds(at, CR), :]], axis=1)
                put(base + level, c, kept * full(base + level, c) + added)

    def local_part(trip, chunk):
        base = base_level(chunk)

        @pl.when(chunk == 0)
        def _():
            above[...] = jnp.zeros_like(above)

        for level in reversed(range(NL)):
            u0 = full(base + level, 0)
            u1 = full(base + level, 1)
            u2 = full(base + level, 2)
            agg = aggregation[0]
            brk = breakup[0]
            flocced = (
                (1.0 - agg) * u0 + agg * u1,
                brk * u0 + (1.0 - agg - brk) * u1 + agg * u2,
                brk * u1 + (1.0 - brk) * u2,
            )
            columns = []
            for c in range(NCLS):
                rate = settling[grid, c]
                value = wet[...] * ((1.0 - rate) * flocced[c] + rate * above[c])
                above[c] = flocced[c]
                outward = diffusivity[0] * value
                k = level * NCLS + c
                put(base + level, c, value - 4.0 * outward)
                flux[trip, k, 8 : 8 + CR] = outward
                row_send[trip, 0, pl.ds(k, 1), :] = outward[0:1, :]
                row_send[trip, 1, pl.ds(k, 1), :] = outward[CR - 1 : CR, :]
                columns.append(jnp.where(iota((CR, HC), 1) < HC // 2, outward[:, :HC], outward[:, HC:]))

            square = jnp.concatenate(columns + [jnp.zeros((HC - NCLS * CR, HC), F32)], axis=0).T
            col_send[trip, 0, :, level * HC : (level + 1) * HC] = square[0:1]
            col_send[trip, 1, :, level * HC : (level + 1) * HC] = square[HC - 1 : HC]


        for side, device in sides:
            halo_copy(trip, side, device).start()

    def stencil(trip, chunk):
        base = base_level(chunk)
        for side, device in sides:
            halo_arrival(trip, side, device).wait_recv()

        for level in range(NL):
            for c in range(NCLS):
                k = level * NCLS + c
                flux[trip, k, 7:8] = inner[NORTH] * row_recv[trip, 0, pl.ds(k, 1), :]
                flux[trip, k, 8 + CR : 9 + CR] = inner[SOUTH] * row_recv[trip, 1, pl.ds(k, 1), :]
            west = inner[WEST] * col_recv[trip, 0, :, level * HC : (level + 1) * HC]
            east = inner[EAST] * col_recv[trip, 1, :, level * HC : (level + 1) * HC]
            kind = iota((HC, HC), 0)
            square = jnp.where(kind == 0, west, jnp.where(kind == HC - 1, east, 0.0)).T
            lanes = iota((CR, HC), 1)
            lane_ids = iota((CR, CC), 1)
            results = []
            for c in range(NCLS):
                k = level * NCLS + c
                middle = flux[trip, k, 8 : 8 + CR]
                left = jnp.where(lane_ids > 0, pltpu.roll(middle, 1, 1), 0.0)
                right = jnp.where(lane_ids < CC - 1, pltpu.roll(middle, CC - 1, 1), 0.0)
                ends = square[c * CR : (c + 1) * CR]
                ends = jnp.concatenate(
                    [jnp.where(lanes < HC // 2, ends, 0.0), jnp.where(lanes >= HC // 2, ends, 0.0)], axis=1
                )
                results.append(
                    full(base + level, c)
                    + flux[trip, k, 7 : 7 + CR]
                    + flux[trip, k, 9 : 9 + CR]
                    + left
                    + right
                    + ends
                )
            for c in range(NCLS):
                put(base + level, c, results[c])

    def first_sends(trip, chunk):
        @pl.when(is_parent)
        def _():
            send_cross(trip, chunk)

        @pl.when(is_child)
        def _():
            send_up(trip, chunk)

    def stores(chunk):
        base = base_level(chunk)
        return [
            pltpu.make_async_copy(
                state.at[base + level, :, h],
                out.at[0, :, base + level, :, pl.ds(h * HC, HC)],
                store_sem.at[chunk, level, h],
            )
            for level in range(NL)
            for h in range(2)
        ]

    def in_range(trip):
        return (trip >= 0) & (trip < TRIPS)

    @pl.loop(0, TRIPS + LEAD_SEND + LAG)
    def _(tick):
        now = tick - LEAD_SEND

        relaying = now + LEAD_RELAY

        @pl.when(is_relay & in_range(relaying) & jnp.logical_not(short(relaying)))
        def _():
            relay(relaying)

        @pl.when(in_range(now))
        def _():
            chunk = lax.rem(now + CHUNKS, CHUNKS)

            @pl.when(is_parent)
            def _():
                nest_parent(now, chunk)

            @pl.when(is_child)
            def _():
                nest_child(now, chunk)

            local_part(now, chunk)

        @pl.when(now >= LAG)
        def _():
            stencil(now - LAG, lax.rem(now - LAG + CHUNKS, CHUNKS))

        @pl.when(now >= CHUNKS + LAG)
        def _():
            for store in stores(now - LAG - CHUNKS):
                store.start()

        sending = now + LEAD_SEND

        @pl.when(sending < TRIPS)
        def _():
            first_sends(sending, lax.rem(sending, CHUNKS))

        answering = now + LEAD_ANSWER

        @pl.when(is_parent & in_range(answering))
        def _():
            send_down(answering, lax.rem(answering + CHUNKS, CHUNKS))
            forward_up(answering)

    def sent(source, kind, device):
        copy(source, source, kind, 0, device).wait_send()

    for side, device in sides:
        sent(row_send.at[:, side] if side < WEST else col_send.at[:, side - WEST], side, device)

    @pl.when(is_parent)
    def _():
        sent(down_cross_send, RELAY, {"gx": partner})
        sent(up_recv, UP_X, {"gx": partner})
        sent(down_send, DOWN, {"gx": partner})

    @pl.when(is_child)
    def _():
        sent(up_send, UP, {"grid": 0})

    @pl.when(is_relay)
    def _():
        sent(relayed.at[pl.ds(0, TRIPS - SHORTS)], DOWN_X, {"grid": 0})

    @pl.loop(0, CHUNKS)
    def _(chunk):
        for store in stores(chunk):
            store.wait()


def local(adjoint, sea_mask, diffusivity, aggregation, breakup, sponge, settling, *tables):
    hbm = pl.BlockSpec(memory_space=pl.ANY)
    return pl.pallas_call(
        kernel,
        out_shape=jax.ShapeDtypeStruct((1, NCLS, LEV, CR, CC), F32),
        in_specs=[hbm] * 10,
        out_specs=hbm,
        scratch_shapes=[
            pltpu.VMEM((1, CR, CC), jnp.int32),
            pltpu.VMEM((1, CR, CC), F32),
            pltpu.VMEM((1, CR, CC), F32),
            pltpu.VMEM((1, CR, CC), F32),
            pltpu.VMEM((1, CR, CC), F32),
            pltpu.SMEM(settling.shape, F32),
        ]
        + [pltpu.SMEM((t.shape[0], t.shape[2], t.shape[1]), jnp.int32) for t in tables]
        + [
            pltpu.VMEM((LEV, NCLS, 2, CR, HC), F32),
            pltpu.VMEM((TRIPS, NK, CR + 16, CC), F32),
            pltpu.VMEM((NCLS, CR, CC), F32),
            pltpu.VMEM((ROWS, HC), F32),
            pltpu.VMEM((ROWS, HC), F32),
            pltpu.VMEM((CR, CC), F32),
            pltpu.VMEM((CR, CC), F32),
            pltpu.VMEM((NCLS, 2 * SLOTS, 3 * HR, HC), F32),
            pltpu.VMEM((TRIPS, 2, NKP, CC), F32),
            pltpu.VMEM((TRIPS, 2, NKP, CC), F32),
            pltpu.VMEM((TRIPS, 2, 1, WIDE), F32),
            pltpu.VMEM((TRIPS, 2, 1, WIDE), F32),
            pltpu.VMEM((TRIPS, NK, HR, HC), F32),
            pltpu.VMEM((TRIPS, SLOTS, NK, HR, HC), F32),
            pltpu.VMEM((TRIPS, SLOTS, NK, HR, HC), F32),
            pltpu.VMEM((TRIPS, SLOTS, NK, HR, HC), F32),
            pltpu.VMEM((TRIPS, SLOTS, NK, HR, HC), F32),
            pltpu.VMEM((TRIPS, SLOTS, NK, HR, HC), F32),
            pltpu.VMEM((TRIPS, SLOTS, NK, HR, HC), F32),
            pltpu.VMEM((TRIPS, NK, HR, HC), F32),
            pltpu.SemaphoreType.DMA((9,)),
            pltpu.SemaphoreType.DMA((NCLS, 2)),
            pltpu.SemaphoreType.DMA((CHUNKS, NL, 2)),
            pltpu.SemaphoreType.DMA((KINDS,)),
            pltpu.SemaphoreType.DMA((TRIPS, KINDS)),
        ],
        compiler_params=pltpu.CompilerParams(
            collective_id=0, has_side_effects=True, vmem_limit_bytes=60 * 1024 * 1024
        ),
        name="nested_steps",
    )(
        adjoint,
        sea_mask,
        diffusivity,
        aggregation,
        breakup,
        sponge,
        settling,
        *(t.transpose(0, 2, 1) for t in tables),
    ).reshape(1, NCLS * LEV, CR, CC)


def solution(mesh):
    tile = P("grid", "gx", "gy")
    in_specs = (P("grid", None, "gx", "gy"),) + (tile,) * 5 + (P(),) * 4
    return jax.shard_map(
        local, mesh=mesh, in_specs=in_specs, out_specs=P("grid", None, "gx", "gy"), check_vma=False
    )
```

```python
import functools

import jax
import jax.numpy as jnp
from jax import lax
from jax.experimental import pallas as pl
from jax.experimental.pallas import tpu as pltpu
from jax.sharding import PartitionSpec as P

NCLS = 3
LEV = 8
STEPS = 2
CR = 32
CC = 256
HR = 16
HC = 128
SLOTS = 3
relaxation = 0.125

CHUNKS = 8
NL = LEV // CHUNKS
NK = NL * NCLS
NKP = -(-NK // 8) * 8
ROWS = NK * CR
WIDE = NL * HC
TRIPS = STEPS * CHUNKS
MESH = pl.DeviceIdType.MESH
F32 = jnp.float32
BF16 = jnp.bfloat16

NORTH, SOUTH, WEST, EAST, UP, UP_X, RELAY, DOWN_X, DOWN = 0, 1, 2, 3, 4, 7, 8, 9, 10
KINDS = 11
LEAD_FORWARD = 3
SHORT, SHORT_END = 3, 8
SHORTS = SHORT * (SHORT_END // CHUNKS)
LAG = 2
LEAD_SEND, LEAD_ANSWER, LEAD_RELAY = CHUNKS - LAG, 2, 4


def iota(shape, dim):
    return lax.broadcasted_iota(jnp.int32, shape, dim)


def halves(x):
    high = x.astype(BF16)
    return high, (x - high.astype(F32)).astype(BF16)


def exact_dot(x, selector):
    high, low = halves(x)
    return jnp.dot(high, selector, preferred_element_type=F32) + jnp.dot(low, selector, preferred_element_type=F32)


def kernel(
    adjoint,
    sea_mask_in,
    diffusivity_in,
    aggregation_in,
    breakup_in,
    sponge_in,
    settling_in,
    partner_flip_in,
    row_offset_in,
    col_offset_in,
    out,
    sea_mask,
    diffusivity,
    aggregation,
    breakup,
    sponge,
    settling,
    partner_flip,
    row_offset,
    col_offset,
    state,
    flux,
    above,
    low_cols,
    high_cols,
    wet,
    cover,
    placed,
    row_send,
    row_recv,
    col_send,
    col_recv,
    up_send,
    up_recv,
    relayed,
    up_cross,
    down_cross_send,
    down_cross_recv,
    down_send,
    down_recv,
    field_sem,
    load_sem,
    store_sem,
    send_sem,
    recv_sem,
):
    grid = lax.axis_index("grid")
    row = lax.axis_index("gx")
    col = lax.axis_index("gy")
    rows = lax.axis_size("gx")
    cols = lax.axis_size("gy")
    is_parent = grid == 0
    is_child = grid > 0
    is_relay = grid == SLOTS
    behind = lax.rem(col + cols - 2, cols)
    ahead = lax.rem(col + 2, cols)
    partner = row + 1 - 2 * lax.rem(row, 2)
    slot_of = grid - 1
    sides = (
        (NORTH, {"gx": lax.rem(row + rows - 1, rows)}),
        (SOUTH, {"gx": lax.rem(row + 1, rows)}),
        (WEST, {"gy": lax.rem(col + cols - 1, cols)}),
        (EAST, {"gy": lax.rem(col + 1, cols)}),
    )
    inner = [
        jnp.where(joint, 0.0, 1.0) for joint in (row == 0, row == rows - 1, col == 0, col == cols - 1)
    ]

    fields = [
        pltpu.make_async_copy(source, target, field_sem.at[n])
        for n, (source, target) in enumerate(
            (
                (partner_flip_in, partner_flip),
                (row_offset_in, row_offset),
                (col_offset_in, col_offset),
                (settling_in, settling),
                (sponge_in, sponge),
                (sea_mask_in, sea_mask),
                (diffusivity_in, diffusivity),
                (aggregation_in, aggregation),
                (breakup_in, breakup),
            )
        )
    ]
    loads = [
        pltpu.make_async_copy(
            adjoint.at[0, pl.ds(c * LEV, LEV), :, pl.ds(h * HC, HC)], state.at[:, c, h], load_sem.at[c, h]
        )
        for c in range(NCLS)
        for h in range(2)
    ]
    for load in fields[:3] + loads + fields[3:]:
        load.start()

    barrier = pltpu.get_barrier_semaphore()

    def greet(device):
        pl.semaphore_signal(barrier, inc=1, device_id=device, device_id_type=MESH)

    for _, device in sides:
        greet(device)

    @pl.when(is_parent)
    def _():
        for slot in range(SLOTS):
            greet({"grid": slot + 1})
        greet({"grid": SLOTS, "gx": partner, "gy": behind})
        greet({"grid": SLOTS, "gy": behind})

    @pl.when(is_child)
    def _():
        greet({"grid": 0})

    @pl.when(is_relay)
    def _():
        greet({"grid": 0, "gx": partner, "gy": ahead})
        greet({"grid": 0, "gy": ahead})

    placed[...] = jnp.zeros_like(placed)
    for load in fields:
        load.wait()
    wet[...] = sea_mask[0].astype(F32)

    tops = [row_offset[g, col, row] for g in range(SLOTS)] + [row_offset[g, col, partner] for g in range(SLOTS)]
    lefts = [col_offset[g, col, row] for g in range(SLOTS)] + [col_offset[g, col, partner] for g in range(SLOTS)]
    flags = [1 - partner_flip[g, col, row] for g in range(SLOTS)] + [partner_flip[g, col, partner] for g in range(SLOTS)]

    @pl.when(is_parent)
    def _():
        row_ids = iota((CR, CC), 0)
        col_ids = iota((CR, CC), 1)
        total = jnp.zeros((CR, CC), F32)
        for top, left, flag in zip(tops, lefts, flags):
            inside = (row_ids >= top) & (row_ids < top + HR) & (col_ids >= left) & (col_ids < left + HC)
            total = total + jnp.where(inside, flag.astype(F32), 0.0)
        cover[...] = 1.0 - relaxation * total

    pl.semaphore_wait(
        barrier,
        4 + jnp.where(is_parent, SLOTS + 2, 1) + jnp.where(is_relay, 2, 0),
    )
    for load in loads:
        load.wait()

    def copy(source, target, kind, trip, device, landing=None):
        return pltpu.make_async_remote_copy(
            src_ref=source,
            dst_ref=target,
            send_sem=send_sem.at[kind],
            recv_sem=recv_sem.at[trip, kind if landing is None else landing],
            device_id=device,
            device_id_type=MESH,
        )

    def up_copy(trip):
        return copy(up_send.at[trip], up_recv.at[trip, slot_of], UP, trip, {"grid": 0}, UP + slot_of)

    def up_arrival(trip, slot):
        return copy(up_send.at[trip], up_recv.at[trip, slot], UP, trip, {"grid": slot + 1}, UP + slot)

    def up_cross_copy(trip):
        return copy(up_recv.at[trip], up_cross.at[trip], UP_X, trip, {"gx": partner})

    def relay_copy(trip):
        return copy(
            down_cross_send.at[trip], relayed.at[trip], RELAY, trip, {"grid": SLOTS, "gx": partner, "gy": behind}
        )

    def short(trip):
        return (lax.rem(trip, CHUNKS) < SHORT) & (trip < SHORT_END)

    def direct_copy(trip):
        return copy(
            down_cross_send.at[trip], down_cross_recv.at[trip], RELAY, trip, {"gx": partner}, DOWN_X
        )

    def down_cross_copy(trip):
        return copy(relayed.at[trip], down_cross_recv.at[trip], DOWN_X, trip, {"grid": 0, "gy": ahead})

    def down_copy(trip, slot):
        return copy(down_send.at[trip, slot], down_recv.at[trip], DOWN, trip, {"grid": slot + 1})

    def down_arrival(trip):
        return copy(down_send.at[trip, 0], down_recv.at[trip], DOWN, trip, {"grid": 0}, DOWN)

    def halo_copy(trip, side, device):
        if side < WEST:
            return copy(row_send.at[trip, side], row_recv.at[trip, 1 - side], side, trip, device, 1 - side)
        return copy(col_send.at[trip, side - WEST], col_recv.at[trip, EAST - side], side, trip, device, WEST + EAST - side)

    def halo_arrival(trip, side, device):
        if side < WEST:
            return copy(row_send.at[trip, side], row_recv.at[trip, side], side, trip, device, side)
        return copy(col_send.at[trip, side - WEST], col_recv.at[trip, side - WEST], side, trip, device, side)

    def base_level(chunk):
        return LEV - NL * (chunk + 1)

    def full(level, c):
        return jnp.concatenate([state[level, c, 0], state[level, c, 1]], axis=1)

    def put(level, c, values):
        state[level, c, 0] = values[:, :HC]
        state[level, c, 1] = values[:, HC:]

    def cut(level, c, top, left):
        low = state[level, c, 0, pl.ds(top, HR), :]
        high = state[level, c, 1, pl.ds(top, HR), :]
        return pltpu.roll(jnp.where(iota((HR, HC), 1) >= left, low, high), lax.rem(HC - left, HC), 1)

    def send_up(trip, chunk):
        base = base_level(chunk)
        weights = sponge[0]

        def component(level, c):
            product = weights * full(base + level, c)
            at = (level * NCLS + c) * CR
            low_cols[pl.ds(at, CR), :] = product[:, :HC]
            high_cols[pl.ds(at, CR), :] = product[:, HC:]

        for level in range(NL):
            for c in range(NCLS):
                component(level, c)

        half = ROWS // 2
        low = low_cols[pl.ds(0, half, stride=2), :] + low_cols[pl.ds(1, half, stride=2), :]
        high = high_cols[pl.ds(0, half, stride=2), :] + high_cols[pl.ds(1, half, stride=2), :]
        selector = (iota((CC, HC), 0) // 2 == iota((CC, HC), 1)).astype(F32).astype(BF16)
        sums = exact_dot(jnp.concatenate([low, high], axis=1), selector)
        up_send[trip] = sums.reshape(NK, HR, HC)
        up_copy(trip).start()

    def send_cross(trip, chunk):
        base = base_level(chunk)

        for level in range(NL):
            for c in range(NCLS):
                for slot in range(SLOTS):
                    down_cross_send[trip, slot, level * NCLS + c] = cut(
                        base + level, c, tops[SLOTS + slot], lefts[SLOTS + slot]
                    )

        @pl.when(short(trip))
        def _():
            direct_copy(trip).start()

        @pl.when(jnp.logical_not(short(trip)))
        def _():
            relay_copy(trip).start()

    def send_down(trip, chunk):
        base = base_level(chunk)
        down_cross_copy(trip).wait_recv()
        for slot in range(SLOTS):
            keep = flags[slot].astype(F32)

            for level in range(NL):
                for c in range(NCLS):
                    values = cut(base + level, c, tops[slot], lefts[slot])
                    other = down_cross_recv[trip, slot, level * NCLS + c]
                    down_send[trip, slot, level * NCLS + c] = keep * values + (1.0 - keep) * other

            down_copy(trip, slot).start()

    def forward_up(trip):
        for slot in range(SLOTS):
            up_arrival(trip, slot).wait_recv()
        up_cross_copy(trip).start()

    def relay(trip):
        relay_copy(trip).wait_recv()
        down_cross_copy(trip).start()

    def nest_parent(trip, chunk):
        base = base_level(chunk)
        up_cross_copy(trip).wait_recv()
        lanes = iota((8, HC), 1)

        for level in range(NL):
            for c in range(NCLS):
                k = level * NCLS + c
                old = full(base + level, c) * cover[...]
                low = old[:, :HC].reshape(CR // 8, 8, HC)
                high = old[:, HC:].reshape(CR // 8, 8, HC)
                for n in range(2 * SLOTS):
                    source = up_recv if n < SLOTS else up_cross
                    placed[c, n, HR : HR + HR] = pltpu.roll(source[trip, n % SLOTS, k], lax.rem(lefts[n], HC), 1)
                    piece = placed[c, n, pl.ds(HR - tops[n], CR), :].reshape(CR // 8, 8, HC)
                    flag = flags[n].astype(F32)
                    low = low + jnp.where(lanes >= lefts[n], flag, 0.0)[None] * piece
                    high = high + jnp.where(lanes < lefts[n], flag, 0.0)[None] * piece
                state[base + level, c, 0] = low.reshape(CR, HC)
                state[base + level, c, 1] = high.reshape(CR, HC)

    def nest_child(trip, chunk):
        base = base_level(chunk)
        down_arrival(trip).wait_recv()
        selector = jnp.where(iota((HC, CC), 1) // 2 == iota((HC, CC), 0), relaxation / 4.0, 0.0).astype(BF16)
        half = ROWS // 2
        spread = exact_dot(down_recv[trip].reshape(NK * HR, HC), selector)
        for start in (0, 1):
            low_cols[pl.ds(start, half, stride=2), :] = spread[:, :HC]
            high_cols[pl.ds(start, half, stride=2), :] = spread[:, HC:]
        kept = 1.0 - sponge[0]

        for level in range(NL):
            for c in range(NCLS):
                at = (level * NCLS + c) * CR
                added = jnp.concatenate([low_cols[pl.ds(at, CR), :], high_cols[pl.ds(at, CR), :]], axis=1)
                put(base + level, c, kept * full(base + level, c) + added)

    def local_part(trip, chunk):
        base = base_level(chunk)

        @pl.when(chunk == 0)
        def _():
            above[...] = jnp.zeros_like(above)

        for level in reversed(range(NL)):
            u0 = full(base + level, 0)
            u1 = full(base + level, 1)
            u2 = full(base + level, 2)
            agg = aggregation[0]
            brk = breakup[0]
            flocced = (
                (1.0 - agg) * u0 + agg * u1,
                brk * u0 + (1.0 - agg - brk) * u1 + agg * u2,
                brk * u1 + (1.0 - brk) * u2,
            )
            columns = []
            for c in range(NCLS):
                rate = settling[grid, c]
                value = wet[...] * ((1.0 - rate) * flocced[c] + rate * above[c])
                above[c] = flocced[c]
                outward = diffusivity[0] * value
                k = level * NCLS + c
                put(base + level, c, value - 4.0 * outward)
                flux[trip, k, 8 : 8 + CR] = outward
                row_send[trip, 0, pl.ds(k, 1), :] = outward[0:1, :]
                row_send[trip, 1, pl.ds(k, 1), :] = outward[CR - 1 : CR, :]
                columns.append(jnp.where(iota((CR, HC), 1) < HC // 2, outward[:, :HC], outward[:, HC:]))

            square = jnp.concatenate(columns + [jnp.zeros((HC - NCLS * CR, HC), F32)], axis=0).T
            col_send[trip, 0, :, level * HC : (level + 1) * HC] = square[0:1]
            col_send[trip, 1, :, level * HC : (level + 1) * HC] = square[HC - 1 : HC]


        for side, device in sides:
            halo_copy(trip, side, device).start()

    def stencil(trip, chunk):
        base = base_level(chunk)
        for side, device in sides:
            halo_arrival(trip, side, device).wait_recv()

        for level in range(NL):
            for c in range(NCLS):
                k = level * NCLS + c
                flux[trip, k, 7:8] = inner[NORTH] * row_recv[trip, 0, pl.ds(k, 1), :]
                flux[trip, k, 8 + CR : 9 + CR] = inner[SOUTH] * row_recv[trip, 1, pl.ds(k, 1), :]
            west = inner[WEST] * col_recv[trip, 0, :, level * HC : (level + 1) * HC]
            east = inner[EAST] * col_recv[trip, 1, :, level * HC : (level + 1) * HC]
            kind = iota((HC, HC), 0)
            square = jnp.where(kind == 0, west, jnp.where(kind == HC - 1, east, 0.0)).T
            lanes = iota((CR, HC), 1)
            lane_ids = iota((CR, CC), 1)
            results = []
            for c in range(NCLS):
                k = level * NCLS + c
                middle = flux[trip, k, 8 : 8 + CR]
                left = jnp.where(lane_ids > 0, pltpu.roll(middle, 1, 1), 0.0)
                right = jnp.where(lane_ids < CC - 1, pltpu.roll(middle, CC - 1, 1), 0.0)
                ends = square[c * CR : (c + 1) * CR]
                ends = jnp.concatenate(
                    [jnp.where(lanes < HC // 2, ends, 0.0), jnp.where(lanes >= HC // 2, ends, 0.0)], axis=1
                )
                results.append(
                    full(base + level, c)
                    + flux[trip, k, 7 : 7 + CR]
                    + flux[trip, k, 9 : 9 + CR]
                    + left
                    + right
                    + ends
                )
            for c in range(NCLS):
                put(base + level, c, results[c])

    def first_sends(trip, chunk):
        @pl.when(is_parent)
        def _():
            send_cross(trip, chunk)

        @pl.when(is_child)
        def _():
            send_up(trip, chunk)

    def stores(chunk):
        base = base_level(chunk)
        return [
            pltpu.make_async_copy(
                state.at[base + level, :, h],
                out.at[0, :, base + level, :, pl.ds(h * HC, HC)],
                store_sem.at[chunk, level, h],
            )
            for level in range(NL)
            for h in range(2)
        ]

    def in_range(trip):
        return (trip >= 0) & (trip < TRIPS)

    @pl.loop(0, TRIPS + LEAD_SEND + LAG)
    def _(tick):
        now = tick - LEAD_SEND

        relaying = now + LEAD_RELAY

        @pl.when(is_relay & in_range(relaying) & jnp.logical_not(short(relaying)))
        def _():
            relay(relaying)

        @pl.when(in_range(now))
        def _():
            chunk = lax.rem(now + CHUNKS, CHUNKS)

            @pl.when(is_parent)
            def _():
                nest_parent(now, chunk)

            @pl.when(is_child)
            def _():
                nest_child(now, chunk)

            local_part(now, chunk)

        @pl.when(now >= LAG)
        def _():
            stencil(now - LAG, lax.rem(now - LAG + CHUNKS, CHUNKS))

        @pl.when(now >= CHUNKS + LAG)
        def _():
            for store in stores(now - LAG - CHUNKS):
                store.start()

        sending = now + LEAD_SEND

        @pl.when(sending < TRIPS)
        def _():
            first_sends(sending, lax.rem(sending, CHUNKS))

        forwarding = now + LEAD_FORWARD

        @pl.when(is_parent & in_range(forwarding))
        def _():
            forward_up(forwarding)

        answering = now + LEAD_ANSWER

        @pl.when(is_parent & in_range(answering))
        def _():
            send_down(answering, lax.rem(answering + CHUNKS, CHUNKS))

    def sent(source, kind, device):
        copy(source, source, kind, 0, device).wait_send()

    for side, device in sides:
        sent(row_send.at[:, side] if side < WEST else col_send.at[:, side - WEST], side, device)

    @pl.when(is_parent)
    def _():
        sent(down_cross_send, RELAY, {"gx": partner})
        sent(up_recv, UP_X, {"gx": partner})
        sent(down_send, DOWN, {"gx": partner})

    @pl.when(is_child)
    def _():
        sent(up_send, UP, {"grid": 0})

    @pl.when(is_relay)
    def _():
        sent(relayed.at[pl.ds(0, TRIPS - SHORTS)], DOWN_X, {"grid": 0})

    @pl.loop(0, CHUNKS)
    def _(chunk):
        for store in stores(chunk):
            store.wait()


def local(adjoint, sea_mask, diffusivity, aggregation, breakup, sponge, settling, *tables):
    hbm = pl.BlockSpec(memory_space=pl.ANY)
    return pl.pallas_call(
        kernel,
        out_shape=jax.ShapeDtypeStruct((1, NCLS, LEV, CR, CC), F32),
        in_specs=[hbm] * 10,
        out_specs=hbm,
        scratch_shapes=[
            pltpu.VMEM((1, CR, CC), jnp.int32),
            pltpu.VMEM((1, CR, CC), F32),
            pltpu.VMEM((1, CR, CC), F32),
            pltpu.VMEM((1, CR, CC), F32),
            pltpu.VMEM((1, CR, CC), F32),
            pltpu.SMEM(settling.shape, F32),
        ]
        + [pltpu.SMEM((t.shape[0], t.shape[2], t.shape[1]), jnp.int32) for t in tables]
        + [
            pltpu.VMEM((LEV, NCLS, 2, CR, HC), F32),
            pltpu.VMEM((TRIPS, NK, CR + 16, CC), F32),
            pltpu.VMEM((NCLS, CR, CC), F32),
            pltpu.VMEM((ROWS, HC), F32),
            pltpu.VMEM((ROWS, HC), F32),
            pltpu.VMEM((CR, CC), F32),
            pltpu.VMEM((CR, CC), F32),
            pltpu.VMEM((NCLS, 2 * SLOTS, 3 * HR, HC), F32),
            pltpu.VMEM((TRIPS, 2, NKP, CC), F32),
            pltpu.VMEM((TRIPS, 2, NKP, CC), F32),
            pltpu.VMEM((TRIPS, 2, 1, WIDE), F32),
            pltpu.VMEM((TRIPS, 2, 1, WIDE), F32),
            pltpu.VMEM((TRIPS, NK, HR, HC), F32),
            pltpu.VMEM((TRIPS, SLOTS, NK, HR, HC), F32),
            pltpu.VMEM((TRIPS, SLOTS, NK, HR, HC), F32),
            pltpu.VMEM((TRIPS, SLOTS, NK, HR, HC), F32),
            pltpu.VMEM((TRIPS, SLOTS, NK, HR, HC), F32),
            pltpu.VMEM((TRIPS, SLOTS, NK, HR, HC), F32),
            pltpu.VMEM((TRIPS, SLOTS, NK, HR, HC), F32),
            pltpu.VMEM((TRIPS, NK, HR, HC), F32),
            pltpu.SemaphoreType.DMA((9,)),
            pltpu.SemaphoreType.DMA((NCLS, 2)),
            pltpu.SemaphoreType.DMA((CHUNKS, NL, 2)),
            pltpu.SemaphoreType.DMA((KINDS,)),
            pltpu.SemaphoreType.DMA((TRIPS, KINDS)),
        ],
        compiler_params=pltpu.CompilerParams(
            collective_id=0, has_side_effects=True, vmem_limit_bytes=60 * 1024 * 1024
        ),
        name="nested_steps",
    )(
        adjoint,
        sea_mask,
        diffusivity,
        aggregation,
        breakup,
        sponge,
        settling,
        *(t.transpose(0, 2, 1) for t in tables),
    ).reshape(1, NCLS * LEV, CR, CC)


def solution(mesh):
    tile = P("grid", "gx", "gy")
    in_specs = (P("grid", None, "gx", "gy"),) + (tile,) * 5 + (P(),) * 4
    return jax.shard_map(
        local, mesh=mesh, in_specs=in_specs, out_specs=P("grid", None, "gx", "gy"), check_vma=False
    )
```

```python
import functools

import jax
import jax.numpy as jnp
from jax import lax
from jax.experimental import pallas as pl
from jax.experimental.pallas import tpu as pltpu
from jax.sharding import PartitionSpec as P

NCLS = 3
LEV = 8
STEPS = 2
CR = 32
CC = 256
HR = 16
HC = 128
SLOTS = 3
relaxation = 0.125

CHUNKS = 8
NL = LEV // CHUNKS
NK = NL * NCLS
NKP = -(-NK // 8) * 8
ROWS = NK * CR
WIDE = NL * HC
TRIPS = STEPS * CHUNKS
MESH = pl.DeviceIdType.MESH
F32 = jnp.float32
BF16 = jnp.bfloat16

NORTH, SOUTH, WEST, EAST, UP, UP_X, RELAY, DOWN_X, DOWN = 0, 1, 2, 3, 4, 7, 8, 9, 10
KINDS = 11
LEAD_FORWARD = 4
SHORT, SHORT_END = 3, 8
SHORTS = SHORT * (SHORT_END // CHUNKS)
LAG = 2
LEAD_SEND, LEAD_ANSWER, LEAD_RELAY = CHUNKS - LAG, 2, 4


def iota(shape, dim):
    return lax.broadcasted_iota(jnp.int32, shape, dim)


def halves(x):
    high = x.astype(BF16)
    return high, (x - high.astype(F32)).astype(BF16)


def exact_dot(x, selector):
    high, low = halves(x)
    return jnp.dot(high, selector, preferred_element_type=F32) + jnp.dot(low, selector, preferred_element_type=F32)


def kernel(
    adjoint,
    sea_mask_in,
    diffusivity_in,
    aggregation_in,
    breakup_in,
    sponge_in,
    settling_in,
    partner_flip_in,
    row_offset_in,
    col_offset_in,
    out,
    sea_mask,
    diffusivity,
    aggregation,
    breakup,
    sponge,
    settling,
    partner_flip,
    row_offset,
    col_offset,
    state,
    flux,
    above,
    low_cols,
    high_cols,
    wet,
    cover,
    placed,
    row_send,
    row_recv,
    col_send,
    col_recv,
    up_send,
    up_recv,
    relayed,
    up_cross,
    down_cross_send,
    down_cross_recv,
    down_send,
    down_recv,
    field_sem,
    load_sem,
    store_sem,
    send_sem,
    recv_sem,
):
    grid = lax.axis_index("grid")
    row = lax.axis_index("gx")
    col = lax.axis_index("gy")
    rows = lax.axis_size("gx")
    cols = lax.axis_size("gy")
    is_parent = grid == 0
    is_child = grid > 0
    is_relay = grid == SLOTS
    behind = lax.rem(col + cols - 2, cols)
    ahead = lax.rem(col + 2, cols)
    partner = row + 1 - 2 * lax.rem(row, 2)
    slot_of = grid - 1
    sides = (
        (NORTH, {"gx": lax.rem(row + rows - 1, rows)}),
        (SOUTH, {"gx": lax.rem(row + 1, rows)}),
        (WEST, {"gy": lax.rem(col + cols - 1, cols)}),
        (EAST, {"gy": lax.rem(col + 1, cols)}),
    )
    inner = [
        jnp.where(joint, 0.0, 1.0) for joint in (row == 0, row == rows - 1, col == 0, col == cols - 1)
    ]

    fields = [
        pltpu.make_async_copy(source, target, field_sem.at[n])
        for n, (source, target) in enumerate(
            (
                (partner_flip_in, partner_flip),
                (row_offset_in, row_offset),
                (col_offset_in, col_offset),
                (settling_in, settling),
                (sponge_in, sponge),
                (sea_mask_in, sea_mask),
                (diffusivity_in, diffusivity),
                (aggregation_in, aggregation),
                (breakup_in, breakup),
            )
        )
    ]
    loads = [
        pltpu.make_async_copy(
            adjoint.at[0, pl.ds(c * LEV, LEV), :, pl.ds(h * HC, HC)], state.at[:, c, h], load_sem.at[c, h]
        )
        for c in range(NCLS)
        for h in range(2)
    ]
    for load in fields[:3] + loads + fields[3:]:
        load.start()

    barrier = pltpu.get_barrier_semaphore()

    def greet(device):
        pl.semaphore_signal(barrier, inc=1, device_id=device, device_id_type=MESH)

    for _, device in sides:
        greet(device)

    @pl.when(is_parent)
    def _():
        for slot in range(SLOTS):
            greet({"grid": slot + 1})
        greet({"grid": SLOTS, "gx": partner, "gy": behind})
        greet({"grid": SLOTS, "gy": behind})

    @pl.when(is_child)
    def _():
        greet({"grid": 0})

    @pl.when(is_relay)
    def _():
        greet({"grid": 0, "gx": partner, "gy": ahead})
        greet({"grid": 0, "gy": ahead})

    placed[...] = jnp.zeros_like(placed)
    for load in fields:
        load.wait()
    wet[...] = sea_mask[0].astype(F32)

    tops = [row_offset[g, col, row] for g in range(SLOTS)] + [row_offset[g, col, partner] for g in range(SLOTS)]
    lefts = [col_offset[g, col, row] for g in range(SLOTS)] + [col_offset[g, col, partner] for g in range(SLOTS)]
    flags = [1 - partner_flip[g, col, row] for g in range(SLOTS)] + [partner_flip[g, col, partner] for g in range(SLOTS)]

    @pl.when(is_parent)
    def _():
        row_ids = iota((CR, CC), 0)
        col_ids = iota((CR, CC), 1)
        total = jnp.zeros((CR, CC), F32)
        for top, left, flag in zip(tops, lefts, flags):
            inside = (row_ids >= top) & (row_ids < top + HR) & (col_ids >= left) & (col_ids < left + HC)
            total = total + jnp.where(inside, flag.astype(F32), 0.0)
        cover[...] = 1.0 - relaxation * total

    pl.semaphore_wait(
        barrier,
        4 + jnp.where(is_parent, SLOTS + 2, 1) + jnp.where(is_relay, 2, 0),
    )
    for load in loads:
        load.wait()

    def copy(source, target, kind, trip, device, landing=None):
        return pltpu.make_async_remote_copy(
            src_ref=source,
            dst_ref=target,
            send_sem=send_sem.at[kind],
            recv_sem=recv_sem.at[trip, kind if landing is None else landing],
            device_id=device,
            device_id_type=MESH,
        )

    def up_copy(trip):
        return copy(up_send.at[trip], up_recv.at[trip, slot_of], UP, trip, {"grid": 0}, UP + slot_of)

    def up_arrival(trip, slot):
        return copy(up_send.at[trip], up_recv.at[trip, slot], UP, trip, {"grid": slot + 1}, UP + slot)

    def up_cross_copy(trip):
        return copy(up_recv.at[trip], up_cross.at[trip], UP_X, trip, {"gx": partner})

    def relay_copy(trip):
        return copy(
            down_cross_send.at[trip], relayed.at[trip], RELAY, trip, {"grid": SLOTS, "gx": partner, "gy": behind}
        )

    def short(trip):
        return (lax.rem(trip, CHUNKS) < SHORT) & (trip < SHORT_END)

    def direct_copy(trip):
        return copy(
            down_cross_send.at[trip], down_cross_recv.at[trip], RELAY, trip, {"gx": partner}, DOWN_X
        )

    def down_cross_copy(trip):
        return copy(relayed.at[trip], down_cross_recv.at[trip], DOWN_X, trip, {"grid": 0, "gy": ahead})

    def down_copy(trip, slot):
        return copy(down_send.at[trip, slot], down_recv.at[trip], DOWN, trip, {"grid": slot + 1})

    def down_arrival(trip):
        return copy(down_send.at[trip, 0], down_recv.at[trip], DOWN, trip, {"grid": 0}, DOWN)

    def halo_copy(trip, side, device):
        if side < WEST:
            return copy(row_send.at[trip, side], row_recv.at[trip, 1 - side], side, trip, device, 1 - side)
        return copy(col_send.at[trip, side - WEST], col_recv.at[trip, EAST - side], side, trip, device, WEST + EAST - side)

    def halo_arrival(trip, side, device):
        if side < WEST:
            return copy(row_send.at[trip, side], row_recv.at[trip, side], side, trip, device, side)
        return copy(col_send.at[trip, side - WEST], col_recv.at[trip, side - WEST], side, trip, device, side)

    def base_level(chunk):
        return LEV - NL * (chunk + 1)

    def full(level, c):
        return jnp.concatenate([state[level, c, 0], state[level, c, 1]], axis=1)

    def put(level, c, values):
        state[level, c, 0] = values[:, :HC]
        state[level, c, 1] = values[:, HC:]

    def cut(level, c, top, left):
        low = state[level, c, 0, pl.ds(top, HR), :]
        high = state[level, c, 1, pl.ds(top, HR), :]
        return pltpu.roll(jnp.where(iota((HR, HC), 1) >= left, low, high), lax.rem(HC - left, HC), 1)

    def send_up(trip, chunk):
        base = base_level(chunk)
        weights = sponge[0]

        def component(level, c):
            product = weights * full(base + level, c)
            at = (level * NCLS + c) * CR
            low_cols[pl.ds(at, CR), :] = product[:, :HC]
            high_cols[pl.ds(at, CR), :] = product[:, HC:]

        for level in range(NL):
            for c in range(NCLS):
                component(level, c)

        half = ROWS // 2
        low = low_cols[pl.ds(0, half, stride=2), :] + low_cols[pl.ds(1, half, stride=2), :]
        high = high_cols[pl.ds(0, half, stride=2), :] + high_cols[pl.ds(1, half, stride=2), :]
        selector = (iota((CC, HC), 0) // 2 == iota((CC, HC), 1)).astype(F32).astype(BF16)
        sums = exact_dot(jnp.concatenate([low, high], axis=1), selector)
        up_send[trip] = sums.reshape(NK, HR, HC)
        up_copy(trip).start()

    def send_cross(trip, chunk):
        base = base_level(chunk)

        for level in range(NL):
            for c in range(NCLS):
                for slot in range(SLOTS):
                    down_cross_send[trip, slot, level * NCLS + c] = cut(
                        base + level, c, tops[SLOTS + slot], lefts[SLOTS + slot]
                    )

        @pl.when(short(trip))
        def _():
            direct_copy(trip).start()

        @pl.when(jnp.logical_not(short(trip)))
        def _():
            relay_copy(trip).start()

    def send_down(trip, chunk):
        base = base_level(chunk)
        down_cross_copy(trip).wait_recv()
        for slot in range(SLOTS):
            keep = flags[slot].astype(F32)

            for level in range(NL):
                for c in range(NCLS):
                    values = cut(base + level, c, tops[slot], lefts[slot])
                    other = down_cross_recv[trip, slot, level * NCLS + c]
                    down_send[trip, slot, level * NCLS + c] = keep * values + (1.0 - keep) * other

            down_copy(trip, slot).start()

    def forward_up(trip):
        for slot in range(SLOTS):
            up_arrival(trip, slot).wait_recv()
        up_cross_copy(trip).start()

    def relay(trip):
        relay_copy(trip).wait_recv()
        down_cross_copy(trip).start()

    def nest_parent(trip, chunk):
        base = base_level(chunk)
        up_cross_copy(trip).wait_recv()
        lanes = iota((8, HC), 1)

        for level in range(NL):
            for c in range(NCLS):
                k = level * NCLS + c
                old = full(base + level, c) * cover[...]
                low = old[:, :HC].reshape(CR // 8, 8, HC)
                high = old[:, HC:].reshape(CR // 8, 8, HC)
                for n in range(2 * SLOTS):
                    source = up_recv if n < SLOTS else up_cross
                    placed[c, n, HR : HR + HR] = pltpu.roll(source[trip, n % SLOTS, k], lax.rem(lefts[n], HC), 1)
                    piece = placed[c, n, pl.ds(HR - tops[n], CR), :].reshape(CR // 8, 8, HC)
                    flag = flags[n].astype(F32)
                    low = low + jnp.where(lanes >= lefts[n], flag, 0.0)[None] * piece
                    high = high + jnp.where(lanes < lefts[n], flag, 0.0)[None] * piece
                state[base + level, c, 0] = low.reshape(CR, HC)
                state[base + level, c, 1] = high.reshape(CR, HC)

    def nest_child(trip, chunk):
        base = base_level(chunk)
        down_arrival(trip).wait_recv()
        selector = jnp.where(iota((HC, CC), 1) // 2 == iota((HC, CC), 0), relaxation / 4.0, 0.0).astype(BF16)
        half = ROWS // 2
        spread = exact_dot(down_recv[trip].reshape(NK * HR, HC), selector)
        for start in (0, 1):
            low_cols[pl.ds(start, half, stride=2), :] = spread[:, :HC]
            high_cols[pl.ds(start, half, stride=2), :] = spread[:, HC:]
        kept = 1.0 - sponge[0]

        for level in range(NL):
            for c in range(NCLS):
                at = (level * NCLS + c) * CR
                added = jnp.concatenate([low_cols[pl.ds(at, CR), :], high_cols[pl.ds(at, CR), :]], axis=1)
                put(base + level, c, kept * full(base + level, c) + added)

    def local_part(trip, chunk):
        base = base_level(chunk)

        @pl.when(chunk == 0)
        def _():
            above[...] = jnp.zeros_like(above)

        for level in reversed(range(NL)):
            u0 = full(base + level, 0)
            u1 = full(base + level, 1)
            u2 = full(base + level, 2)
            agg = aggregation[0]
            brk = breakup[0]
            flocced = (
                (1.0 - agg) * u0 + agg * u1,
                brk * u0 + (1.0 - agg - brk) * u1 + agg * u2,
                brk * u1 + (1.0 - brk) * u2,
            )
            columns = []
            for c in range(NCLS):
                rate = settling[grid, c]
                value = wet[...] * ((1.0 - rate) * flocced[c] + rate * above[c])
                above[c] = flocced[c]
                outward = diffusivity[0] * value
                k = level * NCLS + c
                put(base + level, c, value - 4.0 * outward)
                flux[trip, k, 8 : 8 + CR] = outward
                row_send[trip, 0, pl.ds(k, 1), :] = outward[0:1, :]
                row_send[trip, 1, pl.ds(k, 1), :] = outward[CR - 1 : CR, :]
                columns.append(jnp.where(iota((CR, HC), 1) < HC // 2, outward[:, :HC], outward[:, HC:]))

            square = jnp.concatenate(columns + [jnp.zeros((HC - NCLS * CR, HC), F32)], axis=0).T
            col_send[trip, 0, :, level * HC : (level + 1) * HC] = square[0:1]
            col_send[trip, 1, :, level * HC : (level + 1) * HC] = square[HC - 1 : HC]


        for side, device in sides:
            halo_copy(trip, side, device).start()

    def stencil(trip, chunk):
        base = base_level(chunk)
        for side, device in sides:
            halo_arrival(trip, side, device).wait_recv()

        for level in range(NL):
            for c in range(NCLS):
                k = level * NCLS + c
                flux[trip, k, 7:8] = inner[NORTH] * row_recv[trip, 0, pl.ds(k, 1), :]
                flux[trip, k, 8 + CR : 9 + CR] = inner[SOUTH] * row_recv[trip, 1, pl.ds(k, 1), :]
            west = inner[WEST] * col_recv[trip, 0, :, level * HC : (level + 1) * HC]
            east = inner[EAST] * col_recv[trip, 1, :, level * HC : (level + 1) * HC]
            kind = iota((HC, HC), 0)
            square = jnp.where(kind == 0, west, jnp.where(kind == HC - 1, east, 0.0)).T
            lanes = iota((CR, HC), 1)
            lane_ids = iota((CR, CC), 1)
            results = []
            for c in range(NCLS):
                k = level * NCLS + c
                middle = flux[trip, k, 8 : 8 + CR]
                left = jnp.where(lane_ids > 0, pltpu.roll(middle, 1, 1), 0.0)
                right = jnp.where(lane_ids < CC - 1, pltpu.roll(middle, CC - 1, 1), 0.0)
                ends = square[c * CR : (c + 1) * CR]
                ends = jnp.concatenate(
                    [jnp.where(lanes < HC // 2, ends, 0.0), jnp.where(lanes >= HC // 2, ends, 0.0)], axis=1
                )
                results.append(
                    full(base + level, c)
                    + flux[trip, k, 7 : 7 + CR]
                    + flux[trip, k, 9 : 9 + CR]
                    + left
                    + right
                    + ends
                )
            for c in range(NCLS):
                put(base + level, c, results[c])

    def first_sends(trip, chunk):
        @pl.when(is_parent)
        def _():
            send_cross(trip, chunk)

        @pl.when(is_child)
        def _():
            send_up(trip, chunk)

    def stores(chunk):
        base = base_level(chunk)
        return [
            pltpu.make_async_copy(
                state.at[base + level, :, h],
                out.at[0, :, base + level, :, pl.ds(h * HC, HC)],
                store_sem.at[chunk, level, h],
            )
            for level in range(NL)
            for h in range(2)
        ]

    def in_range(trip):
        return (trip >= 0) & (trip < TRIPS)

    @pl.loop(0, TRIPS + LEAD_SEND + LAG)
    def _(tick):
        now = tick - LEAD_SEND

        relaying = now + LEAD_RELAY

        @pl.when(is_relay & in_range(relaying) & jnp.logical_not(short(relaying)))
        def _():
            relay(relaying)

        @pl.when(in_range(now))
        def _():
            chunk = lax.rem(now + CHUNKS, CHUNKS)

            @pl.when(is_parent)
            def _():
                nest_parent(now, chunk)

            @pl.when(is_child)
            def _():
                nest_child(now, chunk)

            local_part(now, chunk)

        @pl.when(now >= LAG)
        def _():
            stencil(now - LAG, lax.rem(now - LAG + CHUNKS, CHUNKS))

        @pl.when(now >= CHUNKS + LAG)
        def _():
            for store in stores(now - LAG - CHUNKS):
                store.start()

        sending = now + LEAD_SEND

        @pl.when(sending < TRIPS)
        def _():
            first_sends(sending, lax.rem(sending, CHUNKS))

        forwarding = now + LEAD_FORWARD

        @pl.when(is_parent & in_range(forwarding))
        def _():
            forward_up(forwarding)

        answering = now + LEAD_ANSWER

        @pl.when(is_parent & in_range(answering))
        def _():
            send_down(answering, lax.rem(answering + CHUNKS, CHUNKS))

    def sent(source, kind, device):
        copy(source, source, kind, 0, device).wait_send()

    for side, device in sides:
        sent(row_send.at[:, side] if side < WEST else col_send.at[:, side - WEST], side, device)

    @pl.when(is_parent)
    def _():
        sent(down_cross_send, RELAY, {"gx": partner})
        sent(up_recv, UP_X, {"gx": partner})
        sent(down_send, DOWN, {"gx": partner})

    @pl.when(is_child)
    def _():
        sent(up_send, UP, {"grid": 0})

    @pl.when(is_relay)
    def _():
        sent(relayed.at[pl.ds(0, TRIPS - SHORTS)], DOWN_X, {"grid": 0})

    @pl.loop(0, CHUNKS)
    def _(chunk):
        for store in stores(chunk):
            store.wait()


def local(adjoint, sea_mask, diffusivity, aggregation, breakup, sponge, settling, *tables):
    hbm = pl.BlockSpec(memory_space=pl.ANY)
    return pl.pallas_call(
        kernel,
        out_shape=jax.ShapeDtypeStruct((1, NCLS, LEV, CR, CC), F32),
        in_specs=[hbm] * 10,
        out_specs=hbm,
        scratch_shapes=[
            pltpu.VMEM((1, CR, CC), jnp.int32),
            pltpu.VMEM((1, CR, CC), F32),
            pltpu.VMEM((1, CR, CC), F32),
            pltpu.VMEM((1, CR, CC), F32),
            pltpu.VMEM((1, CR, CC), F32),
            pltpu.SMEM(settling.shape, F32),
        ]
        + [pltpu.SMEM((t.shape[0], t.shape[2], t.shape[1]), jnp.int32) for t in tables]
        + [
            pltpu.VMEM((LEV, NCLS, 2, CR, HC), F32),
            pltpu.VMEM((TRIPS, NK, CR + 16, CC), F32),
            pltpu.VMEM((NCLS, CR, CC), F32),
            pltpu.VMEM((ROWS, HC), F32),
            pltpu.VMEM((ROWS, HC), F32),
            pltpu.VMEM((CR, CC), F32),
            pltpu.VMEM((CR, CC), F32),
            pltpu.VMEM((NCLS, 2 * SLOTS, 3 * HR, HC), F32),
            pltpu.VMEM((TRIPS, 2, NKP, CC), F32),
            pltpu.VMEM((TRIPS, 2, NKP, CC), F32),
            pltpu.VMEM((TRIPS, 2, 1, WIDE), F32),
            pltpu.VMEM((TRIPS, 2, 1, WIDE), F32),
            pltpu.VMEM((TRIPS, NK, HR, HC), F32),
            pltpu.VMEM((TRIPS, SLOTS, NK, HR, HC), F32),
            pltpu.VMEM((TRIPS, SLOTS, NK, HR, HC), F32),
            pltpu.VMEM((TRIPS, SLOTS, NK, HR, HC), F32),
            pltpu.VMEM((TRIPS, SLOTS, NK, HR, HC), F32),
            pltpu.VMEM((TRIPS, SLOTS, NK, HR, HC), F32),
            pltpu.VMEM((TRIPS, SLOTS, NK, HR, HC), F32),
            pltpu.VMEM((TRIPS, NK, HR, HC), F32),
            pltpu.SemaphoreType.DMA((9,)),
            pltpu.SemaphoreType.DMA((NCLS, 2)),
            pltpu.SemaphoreType.DMA((CHUNKS, NL, 2)),
            pltpu.SemaphoreType.DMA((KINDS,)),
            pltpu.SemaphoreType.DMA((TRIPS, KINDS)),
        ],
        compiler_params=pltpu.CompilerParams(
            collective_id=0, has_side_effects=True, vmem_limit_bytes=60 * 1024 * 1024
        ),
        name="nested_steps",
    )(
        adjoint,
        sea_mask,
        diffusivity,
        aggregation,
        breakup,
        sponge,
        settling,
        *(t.transpose(0, 2, 1) for t in tables),
    ).reshape(1, NCLS * LEV, CR, CC)


def solution(mesh):
    tile = P("grid", "gx", "gy")
    in_specs = (P("grid", None, "gx", "gy"),) + (tile,) * 5 + (P(),) * 4
    return jax.shard_map(
        local, mesh=mesh, in_specs=in_specs, out_specs=P("grid", None, "gx", "gy"), check_vma=False
    )
```
